256 devices in a mesh: row: 32 (over y_hi, z, core), col: 8 (over y_lo, x).
Axes of the slice: x: 4, y: 4 (y_hi: 2, y_lo: 2; y = y_hi * 2 + y_lo), z: 8, core: 2. Of those that a mesh axis runs over, the one named last changes fastest.
Arguments:
- velocity: float32 [6, 3, 16384], P(None, None, ('row', 'col')), may hold values from -3 to 3
- points: float32 [3, 16384], P(None, ('row', 'col')), may hold values from -1 to 1
- panel_area: float32 [16384], P(('row', 'col')), may hold values from 0.00048828125 to 0.0048828125
- self_term: float32 [16384], P(('row', 'col')), may hold values from 0.5 to 4
- near_index: int32 [16384, 128], P('row', 'col'), may hold values from 0 to 2047
- near_weight: float32 [16384, 128], P('row', 'col'), may hold values from -0.5 to 0.5
Outputs:
- density: float32 [6, 3, 16384], P(None, None, ('row', 'col'))
The draws below stay inside these ranges and needn't reach their ends.
Inputs may be any that keep to these rules, and one draw needn't show every extreme that they name: `near_index`: each entry is a place in the source block of its column of 16 entries; places may repeat, and every listing counts.
All inputs are finite; a program needn't handle non-finite values.
Results may differ from the reference program's by a relative error of at most 0.0003.
Values sent between devices are 32-bit elements; how exact they have to be, the bound alone decides.
A program may use at most 128 MiB of HBM per device.

```python
import math
import jax
import jax.numpy as jnp
from jax import lax

PAN_DEV = 64
RHS = 6
NEAR = 16
ITERS = 3
PANELS = 16384
SRC = 2048
N_COL = 8


def panel_centres(key):
    return jax.random.uniform(jax.random.fold_in(key, 11), (3, PANELS), jnp.float32, -1.0, 1.0)


def draw_points(key, part):
    return panel_centres(key)


def draw_velocity(key, part):
    centres = panel_centres(key)
    zeros_row = jnp.zeros((PANELS,), jnp.float32)
    ones_row = jnp.ones((PANELS,), jnp.float32)
    first = centres[0]
    second = centres[1]
    third = centres[2]
    motions = jnp.stack([jnp.stack([ones_row, zeros_row, zeros_row]), jnp.stack([zeros_row, ones_row, zeros_row]), jnp.stack([zeros_row, zeros_row, ones_row]), jnp.stack([zeros_row, -third, second]), jnp.stack([third, zeros_row, -first]), jnp.stack([-second, first, zeros_row])])
    noise_key = jax.random.fold_in(key, 12)
    rough = 0.5 * jax.random.normal(noise_key, (RHS, 3, PANELS), jnp.float32)
    field = motions + rough
    return jnp.clip(field, -3.0, 3.0)


def touch_ends(array, rng, least, high):
    shape = array.shape
    place = [jax.random.randint(jax.random.fold_in(rng, axis), (), 0, shape[axis]) for axis in range(len(shape))]
    array = array.at[tuple(place)].set(least)
    longest = shape.index(max(shape))
    place[longest] = (place[longest] + 1) % shape[longest]
    return array.at[tuple(place)].set(high)


def block_scale(stream_key, shape, pieces, smallest, largest):
    factor_of, own = 1.0, jax.random.fold_in(stream_key, 6)
    for axis_at, shards_of in pieces:
        steps = jnp.exp(jax.random.uniform(jax.random.fold_in(own, axis_at), (shards_of,), jnp.float32, smallest / len(pieces), largest / len(pieces)))
        factor_of = factor_of * jnp.repeat(steps, shape[axis_at] // shards_of).reshape([-1 if axis == axis_at else 1 for axis in range(len(shape))])
    return factor_of


def normal_values(rng, extent, width, bound, shards=(), dtype=jnp.bfloat16):
    level = block_scale(rng, extent, shards, -0.22, 0.18) if shards else 1.0
    array = jax.random.normal(rng, extent, jnp.float32) * width * level
    return jnp.minimum(jnp.maximum(array, -bound), bound).astype(dtype)


def setup_inputs(seed: int = 0) -> dict:
    keys = jax.random.split(jax.random.key(seed), 7)
    velocity = draw_velocity(jax.random.fold_in(keys[6], 71), 0)
    points = draw_points(jax.random.fold_in(keys[6], 71), 0)
    panel_area = jnp.clip(jnp.exp(math.log(0.0048828125) - 2.3025851 * jax.random.uniform(keys[2], (PANELS,), jnp.float32) ** block_scale(keys[2], (PANELS,), ((0, 256),), -0.2, 0.2)), 0.00048828125, 0.0048828125)
    self_term = jnp.clip(jnp.exp(math.log(4.0) - 2.0794415 * jax.random.uniform(keys[3], (PANELS,), jnp.float32) ** block_scale(keys[3], (PANELS,), ((0, 256),), -0.2, 0.2)), 0.5, 4.0)
    near_index = touch_ends(jax.random.randint(keys[4], (PANELS, N_COL * NEAR), 0, SRC), jax.random.fold_in(keys[4], 1), 0, SRC - 1).astype(jnp.int32)
    near_weight = normal_values(keys[5], (PANELS, N_COL * NEAR), 0.1, 0.5, ((0, 32), (1, 8)), jnp.float32)
    return dict(velocity=velocity, points=points, panel_area=panel_area, self_term=self_term, near_index=near_index, near_weight=near_weight)


BLOB_SQ = 0.0025
INV_EIGHT_PI = 1.0 / (8.0 * math.pi)

def build_columns(values, src_points):
    rhs_count = values.shape[0]
    count = values.shape[2]
    inner_prod = lax.optimization_barrier(jnp.sum(src_points[None] * values, axis=1))
    direct_cols = values.reshape(rhs_count * 3, count)
    outer_cols = (src_points[None, :, None, :] * values[:, None, :, :]).reshape(rhs_count * 9, count)
    scaled = (src_points[None] * inner_prod[:, None]).reshape(rhs_count * 3, count)
    return (direct_cols, jnp.concatenate([direct_cols, inner_prod, outer_cols, scaled], axis=0))

def tile_terms(tgt_points, src_points, src_area, direct_cols, columns):
    offsets = tgt_points[:, :, None] - src_points[:, None, :]
    dist_sq = lax.optimization_barrier(jnp.sum(offsets * offsets, axis=0))
    inv_root = lax.rsqrt(dist_sq + BLOB_SQ)
    kernel_two = src_area[None, :] * inv_root * inv_root * inv_root * INV_EIGHT_PI
    kernel_one = (dist_sq + 2.0 * BLOB_SQ) * kernel_two
    dims = (((1,), (1,)), ((), ()))
    near_one = lax.dot_general(direct_cols, kernel_one, dims, precision=lax.Precision.HIGHEST)
    products = lax.dot_general(columns, kernel_two, dims, precision=lax.Precision.HIGHEST)
    rhs_count = direct_cols.shape[0] // 3
    tgt_count = tgt_points.shape[1]
    direct = near_one.reshape(rhs_count, 3, tgt_count)
    along_f = products[:3 * rhs_count].reshape(rhs_count, 3, tgt_count)
    along_g = products[3 * rhs_count:4 * rhs_count]
    along_yf = products[4 * rhs_count:13 * rhs_count].reshape(rhs_count, 3, 3, tgt_count)
    along_yg = products[13 * rhs_count:].reshape(rhs_count, 3, tgt_count)
    x_dot = lax.optimization_barrier(jnp.sum(tgt_points[None] * along_f, axis=1))
    cross_term = lax.optimization_barrier(jnp.sum(tgt_points[None, None] * along_yf, axis=2))
    return direct + tgt_points[None] * (x_dot - along_g)[:, None] - cross_term + along_yg

def solve_small(hessen, start_norm, count):
    zero = jnp.zeros_like(start_norm)
    target = [start_norm] + [zero] * count
    cosines = []
    sines = []
    triangle = {}
    for k in range(count):
        column = [hessen[i, k] for i in range(k + 2)]
        for j in range(k):
            first_val = column[j]
            second_val = column[j + 1]
            column[j] = cosines[j] * first_val + sines[j] * second_val
            column[j + 1] = cosines[j] * second_val - sines[j] * first_val
        radius = jnp.sqrt(column[k] * column[k] + column[k + 1] * column[k + 1])
        cosine = column[k] / radius
        sine = column[k + 1] / radius
        cosines.append(cosine)
        sines.append(sine)
        for i in range(k):
            triangle[i, k] = column[i]
        triangle[k, k] = radius
        target[k + 1] = -sine * target[k]
        target[k] = cosine * target[k]
    coeffs = [None] * count
    for k in range(count - 1, -1, -1):
        accum = target[k]
        for i in range(k + 1, count):
            accum = accum - triangle[k, i] * coeffs[i]
        coeffs[k] = accum / triangle[k, k]
    return coeffs

def reference(velocity, points, panel_area, self_term, near_index, near_weight):
    rhs_count = velocity.shape[0]
    blocks = PANELS // PAN_DEV
    tgt_blocks = points.reshape(3, blocks, PAN_DEV).transpose(1, 0, 2)
    column_id = (jnp.arange(N_COL * NEAR) // NEAR).astype(jnp.int32)
    glob = ((near_index // PAN_DEV * N_COL + column_id[None]) * PAN_DEV + near_index % PAN_DEV).astype(jnp.int32)

    def apply(vector):
        direct_cols, columns = build_columns(vector, points)

        def one_block(tgt):
            return tile_terms(tgt, points, panel_area, direct_cols, columns)
        distant = lax.map(one_block, tgt_blocks)
        distant = distant.transpose(1, 2, 0, 3).reshape(rhs_count, 3, PANELS)
        nearby = lax.optimization_barrier(jnp.sum(vector[:, :, glob] * near_weight[None, None], axis=-1))
        return self_term[None, None] * vector + distant + nearby

    def norm_of(field):
        return jnp.sqrt(lax.optimization_barrier(jnp.sum(field * field, axis=(1, 2))))
    start_norm = norm_of(velocity)
    basis = [velocity / start_norm[:, None, None]]
    hessen = {}
    for k in range(ITERS):
        image = apply(basis[k])
        for j in range(k + 1):
            value = lax.optimization_barrier(jnp.sum(basis[j] * image, axis=(1, 2)))
            hessen[j, k] = value
            image = image - value[:, None, None] * basis[j]
        length = norm_of(image)
        hessen[k + 1, k] = length
        if k + 1 < ITERS:
            basis.append(image / length[:, None, None])
    coeffs = solve_small(hessen, start_norm, ITERS)
    density = coeffs[0][:, None, None] * basis[0]
    for k in range(1, ITERS):
        density = density + coeffs[k][:, None, None] * basis[k]
    return density
```

```python
import functools
import math

import jax
import jax.numpy as jnp
from jax import lax
from jax.experimental import pallas as pl
from jax.experimental.pallas import tpu as pltpu
from jax.sharding import PartitionSpec as P

MESH = pl.DeviceIdType.MESH
ITERS = 3
BLOB_SQ = 0.0025
INV_EIGHT_PI = 1.0 / (8.0 * math.pi)
GROUP = 16
PAN = 64
LOCAL = GROUP * PAN
LISTED = 16
PAIRS = ((0, 0, 0), (1, 1, 1), (2, 2, 2), (0, 1, 3), (0, 2, 4), (1, 2, 5))
FAR_FIRST = (8, 9, 7, 6, 10, 5, 11, 4, 12, 3, 13, 2, 14, 1, 15)
CHUNK = 256
TILE = 128


def kernel(
    pkt0_ref,
    nidx_ref,
    nwt_ref,
    out_ref,
    pkt,
    ag,
    pts,
    rss,
    rsr,
    nidx,
    nwt,
    srcb,
    tgtb,
    nmat,
    wts,
    fld,
    ag_send,
    ag_recv,
    pts_send,
    pts_recv,
    rs_send,
    rs_recv,
    near_send,
    near_recv,
):
    row = lax.axis_index("row")
    col = lax.axis_index("col")
    y_hi = row // GROUP
    q = row % GROUP
    p = y_hi * 8 + col

    def gather_peer(d):
        other = (q + d) % GROUP
        return other, (y_hi * GROUP + other, col)

    def reduce_device(other):
        return ((other // 8) * GROUP + q, other % 8)

    barrier = pltpu.get_barrier_semaphore()
    for d in range(1, GROUP):
        pl.semaphore_signal(barrier, inc=1, device_id=gather_peer(d)[1], device_id_type=MESH)
        pl.semaphore_signal(barrier, inc=1, device_id=reduce_device((p + d) % GROUP), device_id_type=MESH)

    nidx[y_hi] = jnp.transpose(nidx_ref[...])
    nwt[y_hi] = jnp.transpose(nwt_ref[...])
    pl.semaphore_wait(barrier, 2 * (GROUP - 1))

    partner = ((1 - y_hi) * GROUP + q, col)

    def near_copies(slot):
        return [
            pltpu.make_async_remote_copy(
                src_ref=buf.at[slot],
                dst_ref=buf.at[slot],
                send_sem=near_send.at[i],
                recv_sem=near_recv.at[i],
                device_id=partner,
                device_id_type=MESH,
            )
            for i, buf in enumerate((nidx, nwt))
        ]

    def ag_copy(src, k, d, slot):
        return pltpu.make_async_remote_copy(
            src_ref=src,
            dst_ref=ag.at[k, slot],
            send_sem=ag_send.at[k, d],
            recv_sem=ag_recv.at[k, slot],
            device_id=gather_peer(d)[1],
            device_id_type=MESH,
        )

    def pts_copy(d, slot):
        return pltpu.make_async_remote_copy(
            src_ref=pkt0_ref,
            dst_ref=pts.at[slot],
            send_sem=pts_send.at[d],
            recv_sem=pts_recv.at[slot],
            device_id=reduce_device((p + d) % GROUP),
            device_id_type=MESH,
        )

    def rs_copy(k, other, slot, send_slot):
        return pltpu.make_async_remote_copy(
            src_ref=rss.at[k, other],
            dst_ref=rsr.at[k, slot],
            send_sem=rs_send.at[k, send_slot],
            recv_sem=rs_recv.at[k, slot],
            device_id=reduce_device(other),
            device_id_type=MESH,
        )

    for d in FAR_FIRST:
        ag_copy(pkt0_ref, 0, d, q).start()
        pts_copy(d, p).start()
    for copy in near_copies(y_hi):
        copy.start()
    ag[0, q] = pkt0_ref[...]
    pts[p] = pkt0_ref[...]

    def near_half(half):
        def one(step, carry):
            tile = step // 16
            rows = step % 16
            lanes = pl.ds(pl.multiple_of(tile * TILE, TILE), TILE)
            place = lax.broadcasted_iota(jnp.int32, (64, TILE), 0) + (rows * 64 + y_hi * LOCAL)
            acc = jnp.zeros((64, TILE), jnp.float32)
            for k in range(LISTED):
                idx = nidx[half, pl.ds(k, 1), lanes]
                wt = nwt[half, pl.ds(k, 1), lanes]
                acc = acc + jnp.where(place == idx, wt, 0.0)
            nmat[
                pl.ds(pl.multiple_of(rows * 64, 64), 64),
                pl.ds(pl.multiple_of(half * 512 + tile * TILE, TILE), TILE),
            ] = acc
            return carry

        lax.fori_loop(0, 64, one, 0)

    near_half(y_hi)
    for copy in near_copies(1 - y_hi):
        copy.wait_recv()
    near_half(1 - y_hi)

    lane = lax.broadcasted_iota(jnp.int32, (8, TILE), 1)
    low = lane < PAN
    wide = lax.broadcasted_iota(jnp.int32, (8, 2 * TILE), 1)
    body_lanes = wide < 3 * PAN

    def swap(x):
        return pltpu.roll(x, PAN, 1)

    def join(first, second):
        a, c = first[:, :TILE], first[:, TILE:]
        b, e = second[:, :TILE], second[:, TILE:]
        return (
            jnp.where(low, a, swap(b)),
            jnp.where(low, swap(a), b),
            jnp.where(low, c, swap(e)),
        )

    def wait_gather(k):
        for d in range(1, GROUP):
            other = (q + d) % GROUP
            ag_copy(pkt0_ref, k, d, other).wait_recv()

    wait_gather(0)
    for d in range(1, GROUP):
        pts_copy(d, (p + d) % GROUP).wait_recv()

    for s in range(GROUP):
        for half in range(2):
            line = ag[0, s, 6:7, half * TILE : (half + 1) * TILE]
            flipped = jnp.transpose(jnp.broadcast_to(line, (TILE, TILE)))
            if half == 0:
                srcb[0, s * PAN : (s + 1) * PAN] = flipped[:PAN]
                srcb[1, s * PAN : (s + 1) * PAN] = flipped[PAN:]
            else:
                srcb[2, s * PAN : (s + 1) * PAN] = flipped[:PAN]
                srcb[3, s * PAN : (s + 1) * PAN] = flipped[PAN:] * INV_EIGHT_PI
    for m in range(GROUP // 2):
        for a, tile in enumerate(join(pts[2 * m], pts[2 * m + 1])):
            tgtb[a, :, m * TILE : (m + 1) * TILE] = jnp.broadcast_to(tile[6:7], (16, TILE))

    def build(chunk):
        def one(step, carry):
            rows = pl.ds(pl.multiple_of(step * 16, 16), 16)
            source = [srcb[i, rows, :] for i in range(4)]
            for t in range(CHUNK // TILE):
                lanes = pl.ds(pl.multiple_of(chunk * CHUNK + t * TILE, TILE), TILE)
                off = [tgtb[a, :, lanes] - source[a] for a in range(3)]
                dist = off[0] * off[0] + off[1] * off[1] + off[2] * off[2]
                inv = lax.rsqrt(dist + BLOB_SQ)
                two = source[3] * inv * inv * inv
                one_near = (dist + 2.0 * BLOB_SQ) * two + nmat[rows, lanes]
                scaled = [two * v for v in off]
                for a, b, block in PAIRS:
                    value = scaled[a] * off[b]
                    if a == b:
                        value = value + one_near
                    high = value.astype(jnp.bfloat16)
                    wts[block, 0, rows, lanes] = high
                    wts[block, 1, rows, lanes] = (value - high.astype(jnp.float32)).astype(jnp.bfloat16)
            return carry

        lax.fori_loop(0, LOCAL // 16, one, 0)

    def fill_fields(k):
        for m in range(GROUP // 2):
            for a, tile in enumerate(join(ag[k, 2 * m], ag[k, 2 * m + 1])):
                high = tile.astype(jnp.bfloat16).astype(jnp.float32)
                fld[a, :, m * TILE : (m + 1) * TILE] = jnp.concatenate([high, tile - high], axis=0).astype(jnp.bfloat16)

    def group_dots(k):
        if k == 0:
            total = jnp.zeros((8, 2 * TILE), jnp.float32)
            for s in range(GROUP):
                total = total + ag[0, s] * ag[0, s]
            return jnp.broadcast_to(jnp.sum(jnp.where(body_lanes, total, 0.0), axis=1, keepdims=True), (8, TILE))
        total = ag[k, 0, :, TILE:]
        for s in range(1, GROUP):
            total = total + ag[k, s, :, TILE:]
        return total

    def apply(k):
        fill_fields(k)
        riding = group_dots(k)

        def one(step, carry):
            chunk = (p // 4 + 1 + step) % 4
            if k == 0:
                build(chunk)
            lanes = pl.ds(pl.multiple_of(chunk * CHUNK, CHUNK), CHUNK)
            acc = [jnp.zeros((16, CHUNK), jnp.float32) for _ in range(3)]
            for a, b, block in PAIRS:
                for part in range(2):
                    weights = wts[block, part, :, lanes]
                    if a == b:
                        acc[a] = acc[a] + jnp.dot(fld[a], weights, preferred_element_type=jnp.float32)
                    else:
                        both = jnp.dot(
                            jnp.concatenate([fld[a], fld[b]], axis=0), weights, preferred_element_type=jnp.float32
                        )
                        acc[b] = acc[b] + both[:16]
                        acc[a] = acc[a] + both[16:]
            sums = [v[:8] + v[8:] for v in acc]
            for i in range(4):
                t, odd = i // 2, i % 2
                first, second, third = [v[:, t * TILE : (t + 1) * TILE] for v in sums]
                if odd:
                    first, third = swap(first), swap(third)
                else:
                    second = swap(second)
                other = chunk * 4 + i
                rss[k, other, :, :TILE] = jnp.where(low, first, second)
                rss[k, other, :, TILE:] = jnp.where(low, third, riding)

                @pl.when(other != p)
                def _():
                    rs_copy(k, other, p, other).start()

            return carry

        lax.fori_loop(0, 4, one, 0)
        return collect(k)

    def collect(k):
        total = rss[k, p]
        for d in range(1, GROUP):
            other = (p + d) % GROUP
            rs_copy(k, other, other, other).wait_recv()
            total = total + rsr[k, other]
        return total

    def send_packet(k, vector, dots):
        value = jnp.where(body_lanes, vector, 0.0)
        for i, dot in enumerate(dots):
            value = jnp.where(wide == 3 * PAN + i, dot, value)
        pkt[k] = value
        ag[k, q] = value
        for d in FAR_FIRST:
            ag_copy(pkt.at[k], k, d, q).start()

    def inner(a, b):
        return jnp.sum(jnp.where(body_lanes, a * b, 0.0), axis=1, keepdims=True)

    def pick(total, i):
        return total[:, 3 * PAN + i : 3 * PAN + i + 1]

    def length_of(square, whole):
        return jnp.sqrt(jnp.maximum(square, whole * 1e-7))

    own = jnp.where(body_lanes, pkt0_ref[...], 0.0)
    self_term = jnp.broadcast_to(jnp.where(body_lanes, pkt0_ref[...], 0.0)[7:8], (8, 2 * TILE))

    total = apply(0)
    start_norm = jnp.sqrt(pick(total, 0))
    basis0 = own / start_norm
    image0 = (self_term * own + total) / start_norm

    send_packet(1, image0, [inner(basis0, image0), inner(image0, image0)])
    wait_gather(1)
    total = apply(1)
    h00 = pick(total, 0)
    square = pick(total, 1)
    h10 = length_of(square - h00 * h00, square)
    basis1 = (image0 - h00 * basis0) / h10
    image1 = (self_term * image0 + total - h00 * image0) / h10

    send_packet(
        2,
        image1,
        [inner(basis1, basis1), inner(basis0, image1), inner(basis1, image1), inner(image1, image1)],
    )
    wait_gather(2)
    total = apply(2)
    scale = jnp.sqrt(pick(total, 0))
    second_image = (self_term * image1 + total) / scale
    basis1 = basis1 / scale
    image1 = image1 / scale
    h10 = h10 * scale
    h01 = pick(total, 1) / scale
    h11 = pick(total, 2) / (scale * scale)
    square = pick(total, 3) / (scale * scale)
    h21 = length_of(square - h01 * h01 - h11 * h11, square)
    basis2 = (image1 - h01 * basis0 - h11 * basis1) / h21
    image2 = (second_image - h01 * image0 - h11 * image1) / h21

    send_packet(
        3,
        image2,
        [
            inner(basis2, basis2),
            inner(basis0, image2),
            inner(basis1, image2),
            inner(basis2, image2),
            inner(image2, image2),
        ],
    )
    wait_gather(3)
    riding = group_dots(3)
    for d in range(GROUP):
        rss[3, d, :, TILE:] = riding
        rss[3, d, :, :TILE] = riding
    for d in FAR_FIRST:
        other = (p + d) % GROUP
        rs_copy(3, other, p, other).start()
    total = collect(3)
    scale = jnp.sqrt(pick(total, 0))
    basis2 = basis2 / scale
    h21 = h21 * scale
    h02 = pick(total, 1) / scale
    h12 = pick(total, 2) / scale
    h22 = pick(total, 3) / (scale * scale)
    square = pick(total, 4) / (scale * scale)
    h32 = jnp.sqrt(jnp.maximum(square - h02 * h02 - h12 * h12 - h22 * h22, 0.0))

    columns = [[h00, h10], [h01, h11, h21], [h02, h12, h22, h32]]
    target = [start_norm] + [jnp.zeros_like(start_norm)] * ITERS
    turns = []
    for k in range(ITERS):
        column = columns[k]
        for j in range(k):
            cosine, sine = turns[j]
            column[j], column[j + 1] = (
                cosine * column[j] + sine * column[j + 1],
                cosine * column[j + 1] - sine * column[j],
            )
        radius = jnp.sqrt(column[k] * column[k] + column[k + 1] * column[k + 1])
        cosine, sine = column[k] / radius, column[k + 1] / radius
        turns.append((cosine, sine))
        column[k] = radius
        target[k + 1] = -sine * target[k]
        target[k] = cosine * target[k]
    coeffs = [None] * ITERS
    for k in range(ITERS - 1, -1, -1):
        accum = target[k]
        for i in range(k + 1, ITERS):
            accum = accum - columns[i][k] * coeffs[i]
        coeffs[k] = accum / columns[k][k]
    out_ref[...] = coeffs[0] * basis0 + coeffs[1] * basis1 + coeffs[2] * basis2

    for copy in near_copies(y_hi):
        copy.wait_send()
    for d in range(1, GROUP):
        ag_copy(pkt0_ref, 0, d, q).wait_send()
        pts_copy(d, p).wait_send()
        for k in range(1, ITERS + 1):
            ag_copy(pkt.at[k], k, d, q).wait_send()
        for k in range(ITERS + 1):
            other = (p + d) % GROUP
            rs_copy(k, other, p, other).wait_send()


def body(velocity, points, panel_area, self_term, near_index, near_weight):
    rhs = velocity.shape[0]
    top = jnp.pad(velocity.reshape(rhs, 3 * PAN), ((0, 0), (0, PAN)))
    places = jnp.concatenate([points.reshape(1, 3 * PAN), panel_area.reshape(1, PAN)], axis=1)
    own = jnp.concatenate([self_term] * 4).reshape(1, 4 * PAN)
    packet = jnp.concatenate([top, places, own], axis=0)
    rounds = ITERS + 1
    vmem = pl.BlockSpec(memory_space=pltpu.VMEM)
    result = pl.pallas_call(
        kernel,
        out_shape=jax.ShapeDtypeStruct((8, 4 * PAN), jnp.float32),
        in_specs=[vmem] * 3,
        out_specs=vmem,
        scratch_shapes=[
            pltpu.VMEM((rounds, 8, 4 * PAN), jnp.float32),
            pltpu.VMEM((rounds, GROUP, 8, 4 * PAN), jnp.float32),
            pltpu.VMEM((GROUP, 8, 4 * PAN), jnp.float32),
            pltpu.VMEM((rounds, GROUP, 8, 4 * PAN), jnp.float32),
            pltpu.VMEM((rounds, GROUP, 8, 4 * PAN), jnp.float32),
            pltpu.VMEM((2, LISTED, 512), jnp.int32),
            pltpu.VMEM((2, LISTED, 512), jnp.float32),
            pltpu.VMEM((4, LOCAL, TILE), jnp.float32),
            pltpu.VMEM((3, 16, LOCAL), jnp.float32),
            pltpu.VMEM((LOCAL, LOCAL), jnp.float32),
            pltpu.VMEM((6, 2, LOCAL, LOCAL), jnp.bfloat16),
            pltpu.VMEM((3, 16, LOCAL), jnp.bfloat16),
            pltpu.SemaphoreType.DMA((rounds, GROUP)),
            pltpu.SemaphoreType.DMA((rounds, GROUP)),
            pltpu.SemaphoreType.DMA((GROUP,)),
            pltpu.SemaphoreType.DMA((GROUP,)),
            pltpu.SemaphoreType.DMA((rounds, GROUP)),
            pltpu.SemaphoreType.DMA((rounds, GROUP)),
            pltpu.SemaphoreType.DMA((2,)),
            pltpu.SemaphoreType.DMA((2,)),
        ],
        compiler_params=pltpu.CompilerParams(
            collective_id=0, has_side_effects=True, vmem_limit_bytes=56 * 1024 * 1024
        ),
    )(packet, near_index, near_weight)
    return result[:rhs, : 3 * PAN].reshape(rhs, 3, PAN)


def solution(mesh):
    return jax.shard_map(
        body,
        mesh=mesh,
        in_specs=(
            P(None, None, ("row", "col")),
            P(None, ("row", "col")),
            P(("row", "col")),
            P(("row", "col")),
            P("row", "col"),
            P("row", "col"),
        ),
        out_specs=P(None, None, ("row", "col")),
        check_vma=False,
    )
```

```python
import functools
import math

import jax
import jax.numpy as jnp
from jax import lax
from jax.experimental import pallas as pl
from jax.experimental.pallas import tpu as pltpu
from jax.sharding import PartitionSpec as P

MESH = pl.DeviceIdType.MESH
ITERS = 3
BLOB_SQ = 0.0025
INV_EIGHT_PI = 1.0 / (8.0 * math.pi)
GROUP = 16
PAN = 64
LOCAL = GROUP * PAN
LISTED = 16
MIXED = ((0, 1, 5), (0, 2, 6), (1, 2, 7))
BLOCKS = 8
FAR_FIRST = (8, 9, 7, 6, 10, 5, 11, 4, 12, 3, 13, 2, 14, 1, 15)
CHUNK = 256
TILE = 128
ROUNDS = ITERS + 1
EARLY = 3


def kernel(
    vel_ref,
    points_ref,
    area_ref,
    self_ref,
    nidx_ref,
    nwt_ref,
    out_ref,
    pkt,
    ag,
    pts,
    rss,
    rsr,
    far_idx,
    far_wt,
    digit_a,
    digit_b,
    srcb,
    tgtb,
    nmat,
    wts,
    uacc,
    ag_send,
    ag_recv,
    pts_send,
    pts_recv,
    rs_send,
    rs_recv,
    near_send,
    near_recv,
):
    row = lax.axis_index("row")
    col = lax.axis_index("col")
    y_hi = row // GROUP
    q = row % GROUP
    p = y_hi * 8 + col
    own_rows = q // 4
    own_lanes = p // 4

    def gather_device(other):
        return (y_hi * GROUP + other, col)

    def reduce_device(other):
        return ((other // 8) * GROUP + q, other % 8)

    barrier = pltpu.get_barrier_semaphore()
    for d in range(1, GROUP):
        pl.semaphore_signal(barrier, inc=1, device_id=gather_device((q + d) % GROUP), device_id_type=MESH)
        pl.semaphore_signal(barrier, inc=1, device_id=reduce_device((p + d) % GROUP), device_id_type=MESH)

    pkt[0] = jnp.zeros((8, 2 * TILE), jnp.float32)
    pkt[0, :6, :TILE] = jnp.concatenate([vel_ref[:, 0, :], vel_ref[:, 1, :]], axis=1)
    pkt[0, :6, TILE:] = jnp.concatenate([vel_ref[:, 2, :], jnp.zeros((6, PAN), jnp.float32)], axis=1)
    pkt[0, 6:7, :TILE] = jnp.concatenate([points_ref[0:1], points_ref[1:2]], axis=1)
    pkt[0, 6:7, TILE:] = jnp.concatenate([points_ref[2:3], area_ref[...]], axis=1)

    partner = ((1 - y_hi) * GROUP + q, col)

    def near_copies():
        return [
            pltpu.make_async_remote_copy(
                src_ref=mine,
                dst_ref=theirs,
                send_sem=near_send.at[i],
                recv_sem=near_recv.at[i],
                device_id=partner,
                device_id_type=MESH,
            )
            for i, (mine, theirs) in enumerate(((nidx_ref, far_idx), (nwt_ref, far_wt)))
        ]

    def window(ref, k):
        return ref if k < ITERS else ref.at[:, pl.ds(TILE, TILE)]

    def ag_copy(k, d, slot):
        return pltpu.make_async_remote_copy(
            src_ref=window(pkt.at[k], k),
            dst_ref=window(ag.at[k, slot], k),
            send_sem=ag_send.at[k, d],
            recv_sem=ag_recv.at[k, slot],
            device_id=gather_device((q + d) % GROUP),
            device_id_type=MESH,
        )

    def pts_copy(d, slot):
        return pltpu.make_async_remote_copy(
            src_ref=pkt.at[0],
            dst_ref=pts.at[slot],
            send_sem=pts_send.at[d],
            recv_sem=pts_recv.at[slot],
            device_id=reduce_device((p + d) % GROUP),
            device_id_type=MESH,
        )

    def rs_copy(k, other, slot):
        return pltpu.make_async_remote_copy(
            src_ref=window(rss.at[k, other], k),
            dst_ref=window(rsr.at[k, slot], k),
            send_sem=rs_send.at[k, other],
            recv_sem=rs_recv.at[k, slot],
            device_id=reduce_device(other),
            device_id_type=MESH,
        )

    digit = lax.broadcasted_iota(jnp.int32, (32, TILE), 0)

    def near_tiles(idx_ref, wt_ref, half, first, count):
        def one(step, carry):
            tile = first + step
            lanes = pl.ds(pl.multiple_of(tile * TILE, TILE), TILE)
            out_lanes = pl.ds(pl.multiple_of(half * 512 + tile * TILE, TILE), TILE)
            for k in range(LISTED):
                place = idx_ref[k : k + 1, lanes] - y_hi * LOCAL
                weight = wt_ref[k : k + 1, lanes]
                digit_a[k] = jnp.where(digit == lax.shift_right_arithmetic(place, 5), weight, 0.0)
                digit_b[k] = jnp.where(digit == (place & 31), 1.0, 0.0)
            for group in range(4):
                ones = [digit_b[k, group * 8 : group * 8 + 8, :] for k in range(LISTED)]

                def line(step, carry):
                    for u in range(4):
                        top = step * 4 + u
                        parts = [digit_a[k, pl.ds(top, 1), :] * ones[k] for k in range(LISTED)]
                        while len(parts) > 1:
                            parts = [parts[i] + parts[i + 1] for i in range(0, len(parts), 2)]
                        nmat[pl.ds(pl.multiple_of(top * 32 + group * 8, 8), 8), out_lanes] = parts[0]
                    return carry

                lax.fori_loop(0, 8, line, 0)
            return carry

        lax.fori_loop(0, count, one, 0)

    near_tiles(nidx_ref, nwt_ref, y_hi, 0, EARLY)
    pl.semaphore_wait(barrier, 2 * (GROUP - 1))

    for copy in near_copies():
        copy.start()
    for d in FAR_FIRST:
        pts_copy(d, p).start()
        ag_copy(0, d, q).start()
    ag[0, q] = pkt[0]
    pts[p] = pkt[0]

    near_tiles(nidx_ref, nwt_ref, y_hi, EARLY, 4 - EARLY)
    for copy in near_copies():
        copy.wait_recv()
    near_tiles(far_idx, far_wt, 1 - y_hi, 0, 4)

    lane = lax.broadcasted_iota(jnp.int32, (8, TILE), 1)
    low = lane < PAN
    wide = lax.broadcasted_iota(jnp.int32, (8, 2 * TILE), 1)
    body_lanes = wide < 3 * PAN

    def swap(x):
        return pltpu.roll(x, PAN, 1)

    def join(first, second):
        a, c = first[:, :TILE], first[:, TILE:]
        b, e = second[:, :TILE], second[:, TILE:]
        return (
            jnp.where(low, a, swap(b)),
            jnp.where(low, swap(a), b),
            jnp.where(low, c, swap(e)),
        )

    for d in range(1, GROUP):
        pts_copy(d, (p + d) % GROUP).wait_recv()
    for m in range(GROUP // 2):
        for a, tile in enumerate(join(pts[2 * m], pts[2 * m + 1])):
            tgtb[a, :, m * TILE : (m + 1) * TILE] = jnp.broadcast_to(tile[6:7], (16, TILE))

    def wait_shards(k, rows):
        if rows is None:
            for d in range(1, 4):
                other = own_rows * 4 + (q + d) % 4
                ag_copy(k, d, other).wait_recv()
        else:
            for d in range(4):
                ag_copy(k, d, rows * 4 + d).wait_recv()

    def spread_sources(rows):
        for i in range(4):
            s = rows * 4 + i
            place = pl.ds(pl.multiple_of(s * PAN, PAN), PAN)
            for half in range(2):
                line = ag[0, s, 6:7, half * TILE : (half + 1) * TILE]
                flipped = jnp.transpose(jnp.broadcast_to(line, (TILE, TILE)))
                if half == 0:
                    srcb[0, place] = flipped[:PAN]
                    srcb[1, place] = flipped[PAN:]
                else:
                    srcb[2, place] = flipped[:PAN]
                    srcb[3, place] = flipped[PAN:] * INV_EIGHT_PI

    def build(quarter, chunk):
        def one(step, carry):
            for t in range(CHUNK // TILE):
                rows = pl.ds(pl.multiple_of(quarter * CHUNK + step * 16, 16), 16)
                lanes = pl.ds(pl.multiple_of(chunk * CHUNK + t * TILE, TILE), TILE)
                off = [tgtb[a, :, lanes] - srcb[a, rows, :] for a in range(3)]
                dist = (off[0] * off[0] + off[1] * off[1]) + (off[2] * off[2] + BLOB_SQ)
                inv = lax.rsqrt(dist)
                two = (srcb[3, rows, :] * inv) * (inv * inv)
                near = (dist + BLOB_SQ) * two + nmat[rows, lanes]
                high = near.astype(jnp.bfloat16)
                wts[0, rows, lanes] = high
                wts[1, rows, lanes] = (near - high.astype(jnp.float32)).astype(jnp.bfloat16)
                scaled = [two * v for v in off]
                for a in range(3):
                    wts[2 + a, rows, lanes] = (scaled[a] * off[a]).astype(jnp.bfloat16)
                for a, b, block in MIXED:
                    wts[block, rows, lanes] = (scaled[a] * off[b]).astype(jnp.bfloat16)
            return carry

        lax.fori_loop(0, CHUNK // 16, one, 0)

    def fields(k, rows):
        tiles = [join(ag[k, rows * 4 + 2 * m], ag[k, rows * 4 + 2 * m + 1]) for m in range(2)]
        out = []
        for a in range(3):
            value = jnp.concatenate([tiles[0][a], tiles[1][a]], axis=1)
            high = value.astype(jnp.bfloat16).astype(jnp.float32)
            out.append(jnp.concatenate([high, value - high], axis=0).astype(jnp.bfloat16))
        return out

    def products(field, quarter, chunk):
        rows = pl.ds(pl.multiple_of(quarter * CHUNK, CHUNK), CHUNK)
        lanes = pl.ds(pl.multiple_of(chunk * CHUNK, CHUNK), CHUNK)

        def dot(lhs, block):
            return jnp.dot(lhs, wts[block, rows, lanes], preferred_element_type=jnp.float32)

        stacked = jnp.concatenate(field, axis=0)
        both = dot(stacked, 0) + dot(stacked, 1)
        acc = [both[16 * a : 16 * a + 16] + dot(field[a], 2 + a) for a in range(3)]
        for a, b, block in MIXED:
            both = dot(jnp.concatenate([field[a], field[b]], axis=0), block)
            acc[b] = acc[b] + both[:16]
            acc[a] = acc[a] + both[16:]
        return [v[:8] + v[8:] for v in acc]

    def group_dots(k):
        if k == 0:
            total = jnp.zeros((8, 2 * TILE), jnp.float32)
            for s in range(GROUP):
                total = total + ag[0, s] * ag[0, s]
            return jnp.broadcast_to(jnp.sum(jnp.where(body_lanes, total, 0.0), axis=1, keepdims=True), (8, TILE))
        total = ag[k, 0, :, TILE:]
        for s in range(1, GROUP):
            total = total + ag[k, s, :, TILE:]
        return total

    def apply(k):
        riding = None
        for step, shift in enumerate((0, 1, 3, 2)):
            quarter = (own_rows + shift) % 4
            wait_shards(k, quarter if shift else None)
            if k == 0:
                spread_sources(quarter)
            field = fields(k, quarter)
            if step == 3:
                riding = group_dots(k)
            for turn in (2, 1, 3, 0):
                chunk = (own_lanes + turn) % 4
                if k == 0:
                    build(quarter, chunk)
                sums = products(field, quarter, chunk)
                lanes = pl.ds(pl.multiple_of(chunk * CHUNK, CHUNK), CHUNK)
                if step > 0:
                    sums = [uacc[a, :, lanes] + sums[a] for a in range(3)]
                if step < 3:
                    for a in range(3):
                        uacc[a, :, lanes] = sums[a]
                    continue
                for i in range(4):
                    t, odd = i // 2, i % 2
                    first, second, third = [v[:, t * TILE : (t + 1) * TILE] for v in sums]
                    if odd:
                        first, third = swap(first), swap(third)
                    else:
                        second = swap(second)
                    other = chunk * 4 + i
                    rss[k, other, :, :TILE] = jnp.where(low, first, second)
                    rss[k, other, :, TILE:] = jnp.where(low, third, riding)
                    if turn:
                        rs_copy(k, other, p).start()
                    else:

                        @pl.when(other != p)
                        def _():
                            rs_copy(k, other, p).start()

        return collect(k)

    def collect(k):
        total = rss[k, p]
        for d in range(1, GROUP):
            other = (p + d) % GROUP
            rs_copy(k, other, other).wait_recv()
            total = total + rsr[k, other]
        return total

    def send_packet(k, vector, dots):
        value = jnp.where(body_lanes, vector, 0.0)
        for i, dot in enumerate(dots):
            value = jnp.where(wide == 3 * PAN + i, dot, value)
        pkt[k] = value
        ag[k, q] = value
        for d in FAR_FIRST:
            ag_copy(k, d, q).start()

    def inner(a, b):
        return jnp.sum(jnp.where(body_lanes, a * b, 0.0), axis=1, keepdims=True)

    def pick(total, i):
        return total[:, 3 * PAN + i : 3 * PAN + i + 1]

    def length_of(square, whole):
        return jnp.sqrt(jnp.maximum(square, whole * 1e-7))

    own = jnp.where(body_lanes, pkt[0], 0.0)
    line = jnp.concatenate([self_ref[...], self_ref[...]], axis=1)
    line = jnp.broadcast_to(jnp.concatenate([line, line], axis=1), (8, 2 * TILE))
    self_term = jnp.where(body_lanes, line, 0.0)

    total = apply(0)
    start_norm = jnp.sqrt(pick(total, 0))
    basis0 = own / start_norm
    image0 = (self_term * own + total) / start_norm

    send_packet(1, image0, [inner(basis0, image0), inner(image0, image0)])
    total = apply(1)
    h00 = pick(total, 0)
    square = pick(total, 1)
    h10 = length_of(square - h00 * h00, square)
    basis1 = (image0 - h00 * basis0) / h10
    image1 = (self_term * image0 + total - h00 * image0) / h10

    send_packet(
        2,
        image1,
        [inner(basis1, basis1), inner(basis0, image1), inner(basis1, image1), inner(image1, image1)],
    )
    total = apply(2)
    scale = jnp.sqrt(pick(total, 0))
    second_image = (self_term * image1 + total) / scale
    basis1 = basis1 / scale
    image1 = image1 / scale
    h10 = h10 * scale
    h01 = pick(total, 1) / scale
    h11 = pick(total, 2) / (scale * scale)
    square = pick(total, 3) / (scale * scale)
    h21 = length_of(square - h01 * h01 - h11 * h11, square)
    basis2 = (image1 - h01 * basis0 - h11 * basis1) / h21
    image2 = (second_image - h01 * image0 - h11 * image1) / h21

    send_packet(
        3,
        image2,
        [
            inner(basis2, basis2),
            inner(basis0, image2),
            inner(basis1, image2),
            inner(basis2, image2),
            inner(image2, image2),
        ],
    )
    for d in range(1, GROUP):
        ag_copy(3, d, (q + d) % GROUP).wait_recv()
    riding = group_dots(3)
    for d in range(GROUP):
        rss[3, d, :, TILE:] = riding
    for d in FAR_FIRST:
        rs_copy(3, (p + d) % GROUP, p).start()
    total = collect(3)
    scale = jnp.sqrt(pick(total, 0))
    basis2 = basis2 / scale
    h21 = h21 * scale
    h02 = pick(total, 1) / scale
    h12 = pick(total, 2) / scale
    h22 = pick(total, 3) / (scale * scale)
    square = pick(total, 4) / (scale * scale)
    h32 = jnp.sqrt(jnp.maximum(square - h02 * h02 - h12 * h12 - h22 * h22, 0.0))

    columns = [[h00, h10], [h01, h11, h21], [h02, h12, h22, h32]]
    target = [start_norm] + [jnp.zeros_like(start_norm)] * ITERS
    turns = []
    for k in range(ITERS):
        column = columns[k]
        for j in range(k):
            cosine, sine = turns[j]
            column[j], column[j + 1] = (
                cosine * column[j] + sine * column[j + 1],
                cosine * column[j + 1] - sine * column[j],
            )
        radius = jnp.sqrt(column[k] * column[k] + column[k + 1] * column[k + 1])
        cosine, sine = column[k] / radius, column[k + 1] / radius
        turns.append((cosine, sine))
        column[k] = radius
        target[k + 1] = -sine * target[k]
        target[k] = cosine * target[k]
    coeffs = [None] * ITERS
    for k in range(ITERS - 1, -1, -1):
        accum = target[k]
        for i in range(k + 1, ITERS):
            accum = accum - columns[i][k] * coeffs[i]
        coeffs[k] = accum / columns[k][k]
    density = coeffs[0] * basis0 + coeffs[1] * basis1 + coeffs[2] * basis2
    out_ref[:, 0, :] = density[:6, :PAN]
    out_ref[:, 1, :] = density[:6, PAN : 2 * PAN]
    out_ref[:, 2, :] = density[:6, 2 * PAN : 3 * PAN]

    for copy in near_copies():
        copy.wait_send()
    for d in range(1, GROUP):
        pts_copy(d, p).wait_send()
        for k in range(ROUNDS):
            ag_copy(k, d, q).wait_send()
            rs_copy(k, (p + d) % GROUP, p).wait_send()


def body(velocity, points, panel_area, self_term, near_index, near_weight):
    vmem = pl.BlockSpec(memory_space=pltpu.VMEM)
    rhs = velocity.shape[0]
    return pl.pallas_call(
        kernel,
        out_shape=jax.ShapeDtypeStruct((rhs, 3, PAN), jnp.float32),
        in_specs=[vmem] * 6,
        out_specs=vmem,
        scratch_shapes=[
            pltpu.VMEM((ROUNDS, 8, 4 * PAN), jnp.float32),
            pltpu.VMEM((ROUNDS, GROUP, 8, 4 * PAN), jnp.float32),
            pltpu.VMEM((GROUP, 8, 4 * PAN), jnp.float32),
            pltpu.VMEM((ROUNDS, GROUP, 8, 4 * PAN), jnp.float32),
            pltpu.VMEM((ROUNDS, GROUP, 8, 4 * PAN), jnp.float32),
            pltpu.VMEM((LISTED, 512), jnp.int32),
            pltpu.VMEM((LISTED, 512), jnp.float32),
            pltpu.VMEM((LISTED, 32, TILE), jnp.float32),
            pltpu.VMEM((LISTED, 32, TILE), jnp.float32),
            pltpu.VMEM((4, LOCAL, TILE), jnp.float32),
            pltpu.VMEM((3, 16, LOCAL), jnp.float32),
            pltpu.VMEM((LOCAL, LOCAL), jnp.float32),
            pltpu.VMEM((BLOCKS, LOCAL, LOCAL), jnp.bfloat16),
            pltpu.VMEM((3, 8, LOCAL), jnp.float32),
            pltpu.SemaphoreType.DMA((ROUNDS, GROUP)),
            pltpu.SemaphoreType.DMA((ROUNDS, GROUP)),
            pltpu.SemaphoreType.DMA((GROUP,)),
            pltpu.SemaphoreType.DMA((GROUP,)),
            pltpu.SemaphoreType.DMA((ROUNDS, GROUP)),
            pltpu.SemaphoreType.DMA((ROUNDS, GROUP)),
            pltpu.SemaphoreType.DMA((2,)),
            pltpu.SemaphoreType.DMA((2,)),
        ],
        compiler_params=pltpu.CompilerParams(
            collective_id=0, has_side_effects=True, vmem_limit_bytes=56 * 1024 * 1024
        ),
    )(
        velocity,
        points,
        panel_area.reshape(1, PAN),
        self_term.reshape(1, PAN),
        near_index.T,
        near_weight.T,
    )


def solution(mesh):
    return jax.shard_map(
        body,
        mesh=mesh,
        in_specs=(
            P(None, None, ("row", "col")),
            P(None, ("row", "col")),
            P(("row", "col")),
            P(("row", "col")),
            P("row", "col"),
            P("row", "col"),
        ),
        out_specs=P(None, None, ("row", "col")),
        check_vma=False,
    )
```

```python
import math

import jax
import jax.numpy as jnp
from jax import lax
from jax.experimental import pallas as pl
from jax.experimental.pallas import tpu as pltpu
from jax.sharding import PartitionSpec as P

MESH = pl.DeviceIdType.MESH
ITERS = 3
BLOB_SQ = 0.0025
INV_EIGHT_PI = 1.0 / (8.0 * math.pi)
GROUP = 16
PAN = 64
LOCAL = GROUP * PAN
LISTED = 16
MIXED = ((0, 1, 5), (0, 2, 6), (1, 2, 7))
BLOCKS = 8
FAR_FIRST = (8, 9, 7, 6, 10, 5, 11, 4, 12, 3, 13, 2, 14, 1, 15)
CHUNK = 256
TILE = 128
ROUNDS = ITERS + 1
EARLY = 3


def kernel(
    vel_hbm,
    points_hbm,
    area_hbm,
    self_hbm,
    nidx_hbm,
    nwt_hbm,
    out_ref,
    vel_ref,
    points_ref,
    area_ref,
    self_ref,
    nidx_ref,
    nwt_ref,
    pkt,
    ag,
    pts,
    rss,
    rsr,
    far_idx,
    far_wt,
    digit_a,
    digit_b,
    srcb,
    tgtb,
    nmat,
    wts,
    uacc,
    ag_send,
    ag_recv,
    pts_send,
    pts_recv,
    rs_send,
    rs_recv,
    near_send,
    near_recv,
    load_sem,
):
    row = lax.axis_index("row")
    col = lax.axis_index("col")
    y_hi = row // GROUP
    q = row % GROUP
    p = y_hi * 8 + col
    own_rows = q // 4
    own_lanes = p // 4

    def gather_device(other):
        return (y_hi * GROUP + other, col)

    def reduce_device(other):
        return ((other // 8) * GROUP + q, other % 8)

    barrier = pltpu.get_barrier_semaphore()
    for d in range(1, GROUP):
        pl.semaphore_signal(barrier, inc=1, device_id=gather_device((q + d) % GROUP), device_id_type=MESH)
        pl.semaphore_signal(barrier, inc=1, device_id=reduce_device((p + d) % GROUP), device_id_type=MESH)

    loads = [
        pltpu.make_async_copy(outer, inner, load_sem.at[i])
        for i, (outer, inner) in enumerate(
            (
                (nidx_hbm, nidx_ref),
                (nwt_hbm, nwt_ref),
                (vel_hbm, vel_ref),
                (points_hbm, points_ref),
                (area_hbm, area_ref),
                (self_hbm, self_ref),
            )
        )
    ]
    for load in loads:
        load.start()
    for load in loads:
        load.wait()

    pkt[0] = jnp.zeros((8, 2 * TILE), jnp.float32)
    pkt[0, :6, :TILE] = jnp.concatenate([vel_ref[:, 0, :], vel_ref[:, 1, :]], axis=1)
    pkt[0, :6, TILE:] = jnp.concatenate([vel_ref[:, 2, :], jnp.zeros((6, PAN), jnp.float32)], axis=1)
    pkt[0, 6:7, :TILE] = jnp.concatenate([points_ref[0:1], points_ref[1:2]], axis=1)
    pkt[0, 6:7, TILE:] = jnp.concatenate([points_ref[2:3], area_ref[...]], axis=1)

    partner = ((1 - y_hi) * GROUP + q, col)

    def near_copies():
        return [
            pltpu.make_async_remote_copy(
                src_ref=mine,
                dst_ref=theirs,
                send_sem=near_send.at[i],
                recv_sem=near_recv.at[i],
                device_id=partner,
                device_id_type=MESH,
            )
            for i, (mine, theirs) in enumerate(((nidx_ref, far_idx), (nwt_ref, far_wt)))
        ]

    def window(ref, k):
        return ref if k < ITERS else ref.at[:, pl.ds(TILE, TILE)]

    def ag_copy(k, d, slot):
        return pltpu.make_async_remote_copy(
            src_ref=window(pkt.at[k], k),
            dst_ref=window(ag.at[k, slot], k),
            send_sem=ag_send.at[k],
            recv_sem=ag_recv.at[k, own_rows],
            device_id=gather_device((q + d) % GROUP),
            device_id_type=MESH,
        )

    def pts_copy(d, slot):
        return pltpu.make_async_remote_copy(
            src_ref=pkt.at[0],
            dst_ref=pts.at[slot],
            send_sem=pts_send.at[0],
            recv_sem=pts_recv.at[0],
            device_id=reduce_device((p + d) % GROUP),
            device_id_type=MESH,
        )

    def rs_copy(k, other, slot):
        return pltpu.make_async_remote_copy(
            src_ref=window(rss.at[k, other], k),
            dst_ref=window(rsr.at[k, slot], k),
            send_sem=rs_send.at[k],
            recv_sem=rs_recv.at[k],
            device_id=reduce_device(other),
            device_id_type=MESH,
        )

    def whole(ref, send, recv):
        return pltpu.make_async_remote_copy(
            src_ref=ref,
            dst_ref=ref,
            send_sem=send,
            recv_sem=recv,
            device_id=partner,
            device_id_type=MESH,
        )

    def several(ref, k, first, count):
        if k < ITERS:
            return ref.at[k, pl.ds(first, count)]
        return ref.at[k, pl.ds(first, count), :, pl.ds(TILE, TILE)]

    digit = lax.broadcasted_iota(jnp.int32, (32, TILE), 0)

    def near_tiles(idx_ref, wt_ref, half, first, count):
        def one(step, carry):
            tile = first + step
            lanes = pl.ds(pl.multiple_of(tile * TILE, TILE), TILE)
            for k in range(LISTED):
                place = idx_ref[k : k + 1, lanes] - y_hi * LOCAL
                weight = wt_ref[k : k + 1, lanes]
                digit_a[k] = jnp.where(digit == lax.shift_right_arithmetic(place, 5), weight, 0.0)
                digit_b[k] = jnp.where(digit == (place & 31), 1.0, 0.0)
            for group in range(4):
                ones = [digit_b[k, group * 8 : group * 8 + 8, :] for k in range(LISTED)]

                def line(step, carry):
                    for u in range(8):
                        top = step * 8 + u
                        parts = [digit_a[k, pl.ds(top, 1), :] * ones[k] for k in range(LISTED)]
                        while len(parts) > 1:
                            parts = [parts[i] + parts[i + 1] for i in range(0, len(parts), 2)]
                        nmat[half * 4 + tile, pl.ds(pl.multiple_of(top * 32 + group * 8, 8), 8), :] = parts[0]
                    return carry

                lax.fori_loop(0, 4, line, 0)
            return carry

        lax.fori_loop(0, count, one, 0)

    near_tiles(nidx_ref, nwt_ref, y_hi, 0, EARLY)
    pl.semaphore_wait(barrier, 2 * (GROUP - 1))

    for copy in near_copies():
        copy.start()
    for d in FAR_FIRST:
        pts_copy(d, p).start()
        ag_copy(0, d, q).start()
    ag[0, q] = pkt[0]
    pts[p] = pkt[0]

    near_tiles(nidx_ref, nwt_ref, y_hi, EARLY, 4 - EARLY)
    for copy in near_copies():
        copy.wait_recv()
    near_tiles(far_idx, far_wt, 1 - y_hi, 0, 4)

    lane = lax.broadcasted_iota(jnp.int32, (8, TILE), 1)
    low = lane < PAN
    wide = lax.broadcasted_iota(jnp.int32, (8, 2 * TILE), 1)
    body_lanes = wide < 3 * PAN

    def swap(x):
        return pltpu.roll(x, PAN, 1)

    def join(first, second):
        a, c = first[:, :TILE], first[:, TILE:]
        b, e = second[:, :TILE], second[:, TILE:]
        return (
            jnp.where(low, a, swap(b)),
            jnp.where(low, swap(a), b),
            jnp.where(low, c, swap(e)),
        )

    whole(pts.at[pl.ds(0, GROUP - 1)], pts_send.at[0], pts_recv.at[0]).wait_recv()
    for m in range(GROUP // 2):
        for a, tile in enumerate(join(pts[2 * m], pts[2 * m + 1])):
            tgtb[a, :, m * TILE : (m + 1) * TILE] = jnp.broadcast_to(tile[6:7], (16, TILE))

    def wait_shards(k, rows):
        count = 3 if rows is None else 4
        rows = own_rows if rows is None else rows
        whole(several(ag, k, rows * 4, count), ag_send.at[k], ag_recv.at[k, rows]).wait_recv()

    def spread_sources(rows):
        for i in range(4):
            s = rows * 4 + i
            place = pl.ds(pl.multiple_of(s * PAN, PAN), PAN)
            for half in range(2):
                line = ag[0, s, 6:7, half * TILE : (half + 1) * TILE]
                flipped = jnp.transpose(jnp.broadcast_to(line, (TILE, TILE)))
                if half == 0:
                    srcb[0, place] = flipped[:PAN]
                    srcb[1, place] = flipped[PAN:]
                else:
                    srcb[2, place] = flipped[:PAN]
                    srcb[3, place] = flipped[PAN:] * INV_EIGHT_PI

    def build(quarter, chunk):
        def one(step, carry):
            for h, t in ((0, 0), (0, 1), (1, 0), (1, 1)):
                rows = pl.ds(pl.multiple_of(quarter * CHUNK + step * 32 + h * 16, 16), 16)
                part = slice(t * TILE, (t + 1) * TILE)
                lanes = pl.ds(pl.multiple_of(chunk * CHUNK + t * TILE, TILE), TILE)
                off = [tgtb[a, :, lanes] - srcb[a, rows, :] for a in range(3)]
                dist = (off[0] * off[0] + off[1] * off[1]) + (off[2] * off[2] + BLOB_SQ)
                inv = lax.rsqrt(dist)
                two = (srcb[3, rows, :] * inv) * (inv * inv)
                near = (dist + BLOB_SQ) * two + nmat[chunk * 2 + t, rows, :]
                high = near.astype(jnp.bfloat16)
                wts[0, chunk, rows, part] = high
                wts[1, chunk, rows, part] = (near - high.astype(jnp.float32)).astype(jnp.bfloat16)
                scaled = [two * v for v in off]
                for a in range(3):
                    wts[2 + a, chunk, rows, part] = (scaled[a] * off[a]).astype(jnp.bfloat16)
                for a, b, block in MIXED:
                    wts[block, chunk, rows, part] = (scaled[a] * off[b]).astype(jnp.bfloat16)
            return carry

        lax.fori_loop(0, CHUNK // 32, one, 0)

    def fields(k, rows):
        tiles = [join(ag[k, rows * 4 + 2 * m], ag[k, rows * 4 + 2 * m + 1]) for m in range(2)]
        out = []
        for a in range(3):
            value = jnp.concatenate([tiles[0][a], tiles[1][a]], axis=1)
            high = value.astype(jnp.bfloat16).astype(jnp.float32)
            out.append(jnp.concatenate([high, value - high], axis=0).astype(jnp.bfloat16))
        return out

    def products(field, quarter, chunk):
        rows = pl.ds(pl.multiple_of(quarter * CHUNK, CHUNK), CHUNK)

        def dot(lhs, block):
            return jnp.dot(lhs, wts[block, chunk, rows, :], preferred_element_type=jnp.float32)

        stacked = jnp.concatenate(field, axis=0)
        both = dot(stacked, 0) + dot(stacked, 1)
        acc = [both[16 * a : 16 * a + 16] + dot(field[a], 2 + a) for a in range(3)]
        for a, b, block in MIXED:
            both = dot(jnp.concatenate([field[a], field[b]], axis=0), block)
            acc[b] = acc[b] + both[:16]
            acc[a] = acc[a] + both[16:]
        return [v[:8] + v[8:] for v in acc]

    def group_dots(k):
        if k == 0:
            total = jnp.zeros((8, 2 * TILE), jnp.float32)
            for s in range(GROUP):
                total = total + ag[0, s] * ag[0, s]
            return jnp.broadcast_to(jnp.sum(jnp.where(body_lanes, total, 0.0), axis=1, keepdims=True), (8, TILE))
        total = ag[k, 0, :, TILE:]
        for s in range(1, GROUP):
            total = total + ag[k, s, :, TILE:]
        return total

    def send_sums(k, turn, chunk, sums, riding):
        for i in range(4):
            t, odd = i // 2, i % 2
            first, second, third = [v[:, t * TILE : (t + 1) * TILE] for v in sums]
            if odd:
                first, third = swap(first), swap(third)
            else:
                second = swap(second)
            other = chunk * 4 + i
            rss[k, other, :, :TILE] = jnp.where(low, first, second)
            rss[k, other, :, TILE:] = jnp.where(low, third, riding)
        for i in range(4):
            other = chunk * 4 + i
            if turn:
                rs_copy(k, other, p).start()
            else:

                @pl.when(other != p)
                def _():
                    rs_copy(k, other, p).start()

    def apply(k):
        riding = None
        for step, shift in enumerate((0, 1, 3, 2)):
            quarter = (own_rows + shift) % 4
            wait_shards(k, quarter if shift else None)
            if k == 0:
                spread_sources(quarter)
            field = fields(k, quarter)
            if step == 3:
                riding = group_dots(k)
            for turns in ((2, 1), (3, 0)):
                chunks = [(own_lanes + turn) % 4 for turn in turns]
                if k == 0:
                    for chunk in chunks:
                        build(quarter, chunk)
                results = [products(field, quarter, chunk) for chunk in chunks]
                for turn, chunk, sums in zip(turns, chunks, results):
                    lanes = pl.ds(pl.multiple_of(chunk * CHUNK, CHUNK), CHUNK)
                    if step > 0:
                        sums = [uacc[a, :, lanes] + sums[a] for a in range(3)]
                    if step < 3:
                        for a in range(3):
                            uacc[a, :, lanes] = sums[a]
                    else:
                        send_sums(k, turn, chunk, sums, riding)
        return collect(k)

    def collect(k):
        whole(several(rsr, k, 0, GROUP - 1), rs_send.at[k], rs_recv.at[k]).wait_recv()
        parts = [rss[k, p]] + [rsr[k, (p + d) % GROUP] for d in range(1, GROUP)]
        while len(parts) > 1:
            parts = [parts[i] + parts[i + 1] for i in range(0, len(parts), 2)]
        return parts[0]

    def send_packet(k, vector, dots):
        value = jnp.where(body_lanes, vector, 0.0)
        for i, dot in enumerate(dots):
            value = jnp.where(wide == 3 * PAN + i, dot, value)
        pkt[k] = value
        ag[k, q] = value
        for d in FAR_FIRST:
            ag_copy(k, d, q).start()

    def inner(a, b):
        return jnp.sum(jnp.where(body_lanes, a * b, 0.0), axis=1, keepdims=True)

    def pick(total, i):
        return total[:, 3 * PAN + i : 3 * PAN + i + 1]

    def length_of(square, whole):
        return jnp.sqrt(jnp.maximum(square, whole * 1e-7))

    own = jnp.where(body_lanes, pkt[0], 0.0)
    line = jnp.concatenate([self_ref[...], self_ref[...]], axis=1)
    line = jnp.broadcast_to(jnp.concatenate([line, line], axis=1), (8, 2 * TILE))
    self_term = jnp.where(body_lanes, line, 0.0)

    total = apply(0)
    start_norm = jnp.sqrt(pick(total, 0))
    basis0 = own / start_norm
    image0 = (self_term * own + total) / start_norm

    send_packet(1, image0, [inner(basis0, image0), inner(image0, image0)])
    total = apply(1)
    h00 = pick(total, 0)
    square = pick(total, 1)
    h10 = length_of(square - h00 * h00, square)
    basis1 = (image0 - h00 * basis0) / h10
    image1 = (self_term * image0 + total - h00 * image0) / h10

    send_packet(
        2,
        image1,
        [inner(basis1, basis1), inner(basis0, image1), inner(basis1, image1), inner(image1, image1)],
    )
    total = apply(2)
    scale = jnp.sqrt(pick(total, 0))
    second_image = (self_term * image1 + total) / scale
    basis1 = basis1 / scale
    image1 = image1 / scale
    h10 = h10 * scale
    h01 = pick(total, 1) / scale
    h11 = pick(total, 2) / (scale * scale)
    square = pick(total, 3) / (scale * scale)
    h21 = length_of(square - h01 * h01 - h11 * h11, square)
    basis2 = (image1 - h01 * basis0 - h11 * basis1) / h21
    image2 = (second_image - h01 * image0 - h11 * image1) / h21

    send_packet(
        3,
        image2,
        [
            inner(basis2, basis2),
            inner(basis0, image2),
            inner(basis1, image2),
            inner(basis2, image2),
            inner(image2, image2),
        ],
    )
    for shift in range(4):
        wait_shards(3, (own_rows + shift) % 4 if shift else None)
    riding = group_dots(3)
    for d in range(GROUP):
        rss[3, d, :, TILE:] = riding
    for d in FAR_FIRST:
        rs_copy(3, (p + d) % GROUP, p).start()
    total = collect(3)
    scale = jnp.sqrt(pick(total, 0))
    basis2 = basis2 / scale
    h21 = h21 * scale
    h02 = pick(total, 1) / scale
    h12 = pick(total, 2) / scale
    h22 = pick(total, 3) / (scale * scale)
    square = pick(total, 4) / (scale * scale)
    h32 = jnp.sqrt(jnp.maximum(square - h02 * h02 - h12 * h12 - h22 * h22, 0.0))

    columns = [[h00, h10], [h01, h11, h21], [h02, h12, h22, h32]]
    target = [start_norm] + [jnp.zeros_like(start_norm)] * ITERS
    turns = []
    for k in range(ITERS):
        column = columns[k]
        for j in range(k):
            cosine, sine = turns[j]
            column[j], column[j + 1] = (
                cosine * column[j] + sine * column[j + 1],
                cosine * column[j + 1] - sine * column[j],
            )
        radius = jnp.sqrt(column[k] * column[k] + column[k + 1] * column[k + 1])
        cosine, sine = column[k] / radius, column[k + 1] / radius
        turns.append((cosine, sine))
        column[k] = radius
        target[k + 1] = -sine * target[k]
        target[k] = cosine * target[k]
    coeffs = [None] * ITERS
    for k in range(ITERS - 1, -1, -1):
        accum = target[k]
        for i in range(k + 1, ITERS):
            accum = accum - columns[i][k] * coeffs[i]
        coeffs[k] = accum / columns[k][k]
    density = coeffs[0] * basis0 + coeffs[1] * basis1 + coeffs[2] * basis2
    out_ref[:, 0, :] = density[:6, :PAN]
    out_ref[:, 1, :] = density[:6, PAN : 2 * PAN]
    out_ref[:, 2, :] = density[:6, 2 * PAN : 3 * PAN]

    for copy in near_copies():
        copy.wait_send()
    whole(rss.at[0, pl.ds(0, GROUP - 1)], pts_send.at[0], pts_recv.at[0]).wait_send()
    for k in range(ROUNDS):
        whole(several(rss, k, 0, GROUP - 1), ag_send.at[k], ag_recv.at[k, 0]).wait_send()
        whole(several(rss, k, 0, GROUP - 1), rs_send.at[k], rs_recv.at[k]).wait_send()


def body(velocity, points, panel_area, self_term, near_index, near_weight):
    vmem = pl.BlockSpec(memory_space=pltpu.VMEM)
    rhs = velocity.shape[0]
    return pl.pallas_call(
        kernel,
        out_shape=jax.ShapeDtypeStruct((rhs, 3, PAN), jnp.float32),
        in_specs=[pl.BlockSpec(memory_space=pl.ANY)] * 6,
        out_specs=vmem,
        scratch_shapes=[
            pltpu.VMEM((rhs, 3, PAN), jnp.float32),
            pltpu.VMEM((3, PAN), jnp.float32),
            pltpu.VMEM((1, PAN), jnp.float32),
            pltpu.VMEM((1, PAN), jnp.float32),
            pltpu.VMEM((LISTED, 512), jnp.int32),
            pltpu.VMEM((LISTED, 512), jnp.float32),
            pltpu.VMEM((ROUNDS, 8, 4 * PAN), jnp.float32),
            pltpu.VMEM((ROUNDS, GROUP, 8, 4 * PAN), jnp.float32),
            pltpu.VMEM((GROUP, 8, 4 * PAN), jnp.float32),
            pltpu.VMEM((ROUNDS, GROUP, 8, 4 * PAN), jnp.float32),
            pltpu.VMEM((ROUNDS, GROUP, 8, 4 * PAN), jnp.float32),
            pltpu.VMEM((LISTED, 512), jnp.int32),
            pltpu.VMEM((LISTED, 512), jnp.float32),
            pltpu.VMEM((LISTED, 32, TILE), jnp.float32),
            pltpu.VMEM((LISTED, 32, TILE), jnp.float32),
            pltpu.VMEM((4, LOCAL, TILE), jnp.float32),
            pltpu.VMEM((3, 16, LOCAL), jnp.float32),
            pltpu.VMEM((8, LOCAL, TILE), jnp.float32),
            pltpu.VMEM((BLOCKS, 4, LOCAL, CHUNK), jnp.bfloat16),
            pltpu.VMEM((3, 8, LOCAL), jnp.float32),
            pltpu.SemaphoreType.DMA((ROUNDS,)),
            pltpu.SemaphoreType.DMA((ROUNDS, 4)),
            pltpu.SemaphoreType.DMA((1,)),
            pltpu.SemaphoreType.DMA((1,)),
            pltpu.SemaphoreType.DMA((ROUNDS,)),
            pltpu.SemaphoreType.DMA((ROUNDS,)),
            pltpu.SemaphoreType.DMA((2,)),
            pltpu.SemaphoreType.DMA((2,)),
            pltpu.SemaphoreType.DMA((6,)),
        ],
        compiler_params=pltpu.CompilerParams(
            collective_id=0, has_side_effects=True, vmem_limit_bytes=56 * 1024 * 1024
        ),
    )(
        velocity,
        points,
        panel_area.reshape(1, PAN),
        self_term.reshape(1, PAN),
        near_index.T,
        near_weight.T,
    )


def solution(mesh):
    return jax.shard_map(
        body,
        mesh=mesh,
        in_specs=(
            P(None, None, ("row", "col")),
            P(None, ("row", "col")),
            P(("row", "col")),
            P(("row", "col")),
            P("row", "col"),
            P("row", "col"),
        ),
        out_specs=P(None, None, ("row", "col")),
        check_vma=False,
    )
```

```python
import math

import jax
import jax.numpy as jnp
from jax import lax
from jax.experimental import pallas as pl
from jax.experimental.pallas import tpu as pltpu
from jax.sharding import PartitionSpec as P

MESH = pl.DeviceIdType.MESH
ITERS = 3
BLOB_SQ = 0.0025
INV_EIGHT_PI = 1.0 / (8.0 * math.pi)
GROUP = 16
PAN = 64
LOCAL = GROUP * PAN
LISTED = 16
MIXED = ((0, 1, 5), (0, 2, 6), (1, 2, 7))
BLOCKS = 8
FAR_FIRST = (8, 9, 7, 6, 10, 5, 11, 4, 12, 3, 13, 2, 14, 1, 15)
CHUNK = 256
HALF = 512
PAD = 16
ROWS = 6
TILE = 128
ROUNDS = ITERS + 1
EARLY = 4


def kernel(
    vel_hbm,
    points_hbm,
    area_hbm,
    self_hbm,
    nidx_hbm,
    nwt_hbm,
    out_ref,
    vel_ref,
    points_ref,
    area_ref,
    self_ref,
    nidx_ref,
    nwt_ref,
    pkt,
    ag,
    pts,
    rss,
    rsr,
    far_idx,
    far_wt,
    digit_a,
    digit_b,
    srcb,
    tgtb,
    nmat,
    wts,
    uacc,
    ag_send,
    ag_recv,
    pts_send,
    pts_recv,
    rs_send,
    rs_recv,
    near_send,
    near_recv,
    load_sem,
):
    row = lax.axis_index("row")
    col = lax.axis_index("col")
    y_hi = row // GROUP
    q = row % GROUP
    p = y_hi * 8 + col
    own_rows = q // 4

    def gather_device(other):
        return (y_hi * GROUP + other, col)

    def reduce_device(other):
        return ((other // 8) * GROUP + q, other % 8)

    barrier = pltpu.get_barrier_semaphore()
    for d in range(1, GROUP):
        pl.semaphore_signal(barrier, inc=1, device_id=gather_device((q + d) % GROUP), device_id_type=MESH)
        pl.semaphore_signal(barrier, inc=1, device_id=reduce_device((p + d) % GROUP), device_id_type=MESH)

    loads = [
        pltpu.make_async_copy(outer, inner, load_sem.at[i])
        for i, (outer, inner) in enumerate(
            (
                (nidx_hbm, nidx_ref),
                (nwt_hbm, nwt_ref),
                (vel_hbm, vel_ref),
                (points_hbm, points_ref),
                (area_hbm, area_ref),
                (self_hbm, self_ref),
            )
        )
    ]
    for load in loads:
        load.start()
    for load in loads:
        load.wait()

    spare = [points_ref[0:1], points_ref[1:2], points_ref[2:3], area_ref[...], jnp.zeros((2, PAN), jnp.float32)]
    pkt[0] = jnp.zeros((8, 2 * TILE), jnp.float32)
    pkt[0, :ROWS, :TILE] = jnp.concatenate([vel_ref[:, 0, :], vel_ref[:, 1, :]], axis=1)
    pkt[0, :ROWS, TILE:] = jnp.concatenate([vel_ref[:, 2, :], jnp.concatenate(spare, axis=0)], axis=1)

    partner = ((1 - y_hi) * GROUP + q, col)

    def near_copies():
        return [
            pltpu.make_async_remote_copy(
                src_ref=mine,
                dst_ref=theirs,
                send_sem=near_send.at[i],
                recv_sem=near_recv.at[i],
                device_id=partner,
                device_id_type=MESH,
            )
            for i, (mine, theirs) in enumerate(((nidx_ref, far_idx), (nwt_ref, far_wt)))
        ]

    def window(ref, k):
        return ref.at[pl.ds(0, ROWS)] if k < ITERS else ref.at[pl.ds(0, ROWS), pl.ds(TILE, TILE)]

    def ag_copy(k, d, slot):
        return pltpu.make_async_remote_copy(
            src_ref=window(pkt.at[k], k),
            dst_ref=window(ag.at[k, slot], k),
            send_sem=ag_send.at[k],
            recv_sem=ag_recv.at[k, own_rows],
            device_id=gather_device((q + d) % GROUP),
            device_id_type=MESH,
        )

    def pts_copy(d, slot):
        return pltpu.make_async_remote_copy(
            src_ref=window(pkt.at[0], 0),
            dst_ref=window(pts.at[slot], 0),
            send_sem=pts_send.at[0],
            recv_sem=pts_recv.at[0],
            device_id=reduce_device((p + d) % GROUP),
            device_id_type=MESH,
        )

    def rs_copy(k, other, slot):
        return pltpu.make_async_remote_copy(
            src_ref=window(rss.at[k, other], k),
            dst_ref=window(rsr.at[k, slot], k),
            send_sem=rs_send.at[k],
            recv_sem=rs_recv.at[k],
            device_id=reduce_device(other),
            device_id_type=MESH,
        )

    def whole(ref, send, recv):
        return pltpu.make_async_remote_copy(
            src_ref=ref,
            dst_ref=ref,
            send_sem=send,
            recv_sem=recv,
            device_id=partner,
            device_id_type=MESH,
        )

    def several(ref, k, first, count):
        if k < ITERS:
            return ref.at[k, pl.ds(first, count), pl.ds(0, ROWS)]
        return ref.at[k, pl.ds(first, count), pl.ds(0, ROWS), pl.ds(TILE, TILE)]

    digit = lax.broadcasted_iota(jnp.int32, (32, TILE), 0)

    def near_tiles(idx_ref, wt_ref, half, first, count):
        def one(step, carry):
            tile = first + step
            lanes = pl.ds(pl.multiple_of(tile * TILE, TILE), TILE)
            for k in range(LISTED):
                place = idx_ref[k : k + 1, lanes] - y_hi * LOCAL
                weight = wt_ref[k : k + 1, lanes]
                digit_a[k] = jnp.where(digit == lax.shift_right_arithmetic(place, 5), weight, 0.0)
                digit_b[k] = jnp.where(digit == (place & 31), 1.0, 0.0)
            for group in range(4):
                ones = [digit_b[k, group * 8 : group * 8 + 8, :] for k in range(LISTED)]

                def line(step, carry):
                    for u in range(8):
                        top = step * 8 + u
                        parts = [digit_a[k, pl.ds(top, 1), :] * ones[k] for k in range(LISTED)]
                        while len(parts) > 1:
                            parts = [parts[i] + parts[i + 1] for i in range(0, len(parts), 2)]
                        nmat[half * 4 + tile, pl.ds(pl.multiple_of(top * 32 + group * 8, 8), 8), :] = parts[0]
                    return carry

                lax.fori_loop(0, 4, line, 0)
            return carry

        lax.fori_loop(0, count, one, 0)

    near_tiles(nidx_ref, nwt_ref, y_hi, 0, EARLY)
    pl.semaphore_wait(barrier, 2 * (GROUP - 1))

    for copy in near_copies():
        copy.start()
    for d in FAR_FIRST:
        pts_copy(d, p).start()
        ag_copy(0, d, q).start()
    ag[0, q] = pkt[0]
    pts[p] = pkt[0]

    near_tiles(nidx_ref, nwt_ref, y_hi, EARLY, 4 - EARLY)
    for copy in near_copies():
        copy.wait_recv()
    near_tiles(far_idx, far_wt, 1 - y_hi, 0, 4)

    lane = lax.broadcasted_iota(jnp.int32, (8, TILE), 1)
    low = lane < PAN
    wide = lax.broadcasted_iota(jnp.int32, (8, 2 * TILE), 1)
    body_lanes = wide < 3 * PAN

    def swap(x):
        return pltpu.roll(x, PAN, 1)

    def join(first, second):
        a, c = first[:, :TILE], first[:, TILE:]
        b, e = second[:, :TILE], second[:, TILE:]
        return (
            jnp.where(low, a, swap(b)),
            jnp.where(low, swap(a), b),
            jnp.where(low, c, swap(e)),
        )

    whole(pts.at[pl.ds(0, GROUP - 1), pl.ds(0, ROWS)], pts_send.at[0], pts_recv.at[0]).wait_recv()
    for m in range(GROUP // 2):
        tile = jnp.where(low, swap(pts[2 * m, :, TILE:]), pts[2 * m + 1, :, TILE:])
        for a in range(3):
            tgtb[a, :, m * TILE : (m + 1) * TILE] = jnp.broadcast_to(tile[a : a + 1], (16, TILE))

    def wait_shards(k, rows):
        count = 3 if rows is None else 4
        rows = own_rows if rows is None else rows
        whole(several(ag, k, rows * 4, count), ag_send.at[k], ag_recv.at[k, rows]).wait_recv()

    def spread_sources(rows):
        for i in range(4):
            s = rows * 4 + i
            place = pl.ds(pl.multiple_of(s * PAN, PAN), PAN)
            tile = ag[0, s, :, TILE:]
            moved = swap(tile)
            for pair in range(2):
                line = jnp.where(low[:1], moved[2 * pair : 2 * pair + 1], tile[2 * pair + 1 : 2 * pair + 2])
                flipped = jnp.transpose(jnp.broadcast_to(line, (TILE, TILE)))
                srcb[2 * pair, place] = flipped[:PAN]
                srcb[2 * pair + 1, place] = flipped[PAN:] if pair == 0 else flipped[PAN:] * INV_EIGHT_PI

    def build(quarter, half):
        def one(step, carry):
            rows = pl.ds(pl.multiple_of(quarter * CHUNK + step * 16, 16), 16)
            source = [srcb[i, rows, :] for i in range(4)]
            for t in range(HALF // TILE):
                tile = half * (HALF // TILE) + t
                lanes = pl.ds(pl.multiple_of(tile * TILE, TILE), TILE)
                off = [tgtb[a, :, lanes] - source[a] for a in range(3)]
                dist = (off[0] * off[0] + off[1] * off[1]) + (off[2] * off[2] + BLOB_SQ)
                inv = lax.rsqrt(dist)
                two = (source[3] * inv) * (inv * inv)
                near = (dist + BLOB_SQ) * two + nmat[tile, rows, :]
                high = near.astype(jnp.bfloat16)
                wts[0, tile, rows, :] = high
                wts[1, tile, rows, :] = (near - high.astype(jnp.float32)).astype(jnp.bfloat16)
                scaled = [two * v for v in off]
                for a in range(3):
                    wts[2 + a, tile, rows, :] = (scaled[a] * off[a]).astype(jnp.bfloat16)
                for a, b, block in MIXED:
                    wts[block, tile, rows, :] = (scaled[a] * off[b]).astype(jnp.bfloat16)
            return carry

        lax.fori_loop(0, CHUNK // 16, one, 0)

    def fields(k, rows):
        tiles = [join(ag[k, rows * 4 + 2 * m], ag[k, rows * 4 + 2 * m + 1]) for m in range(2)]
        out = []
        for a in range(3):
            value = jnp.concatenate([tiles[0][a], tiles[1][a]], axis=1)
            high = value.astype(jnp.bfloat16).astype(jnp.float32)
            out.append(jnp.concatenate([high, value - high], axis=0).astype(jnp.bfloat16))
        return out

    def products(field, quarter, half):
        rows = pl.ds(pl.multiple_of(quarter * CHUNK, CHUNK), CHUNK)

        def dot(lhs, block):
            tiles = [wts[block, half * (HALF // TILE) + t, rows, :] for t in range(HALF // TILE)]
            return jnp.dot(lhs, jnp.concatenate(tiles, axis=1), preferred_element_type=jnp.float32)

        stacked = jnp.concatenate(field, axis=0)
        both = dot(stacked, 0) + dot(stacked, 1)
        acc = [both[16 * a : 16 * a + 16] + dot(field[a], 2 + a) for a in range(3)]
        for a, b, block in MIXED:
            both = dot(jnp.concatenate([field[a], field[b]], axis=0), block)
            acc[b] = acc[b] + both[:16]
            acc[a] = acc[a] + both[16:]
        return [v[:8] + v[8:] for v in acc]

    def group_dots(k):
        if k == 0:
            total = jnp.zeros((8, 2 * TILE), jnp.float32)
            for s in range(GROUP):
                total = total + ag[0, s] * ag[0, s]
            return jnp.broadcast_to(jnp.sum(jnp.where(body_lanes, total, 0.0), axis=1, keepdims=True), (8, TILE))
        total = ag[k, 0, :, TILE:]
        for s in range(1, GROUP):
            total = total + ag[k, s, :, TILE:]
        return total

    def send_sums(k, half, near, sums, riding):
        for i in range(8):
            t, odd = i // 2, i % 2
            first, second, third = [v[:, t * TILE : (t + 1) * TILE] for v in sums]
            if odd:
                first, third = swap(first), swap(third)
            else:
                second = swap(second)
            other = half * 8 + i
            rss[k, other, :, :TILE] = jnp.where(low, first, second)
            rss[k, other, :, TILE:] = jnp.where(low, third, riding)
        for i in range(8):
            other = half * 8 + i
            if near:

                @pl.when(other != p)
                def _():
                    rs_copy(k, other, p).start()

            else:
                rs_copy(k, other, p).start()

    def apply(k):
        riding = None
        for step, shift in enumerate((0, 1, 3, 2)):
            quarter = (own_rows + shift) % 4
            wait_shards(k, quarter if shift else None)
            if k == 0:
                spread_sources(quarter)
            field = fields(k, quarter)
            if step == 3:
                riding = group_dots(k)
            for near in range(2):
                half = y_hi if near else 1 - y_hi
                if k == 0:
                    build(quarter, half)
                sums = products(field, quarter, half)
                lanes = pl.ds(pl.multiple_of(half * HALF, HALF), HALF)
                if step > 0:
                    sums = [uacc[a, :, lanes] + sums[a] for a in range(3)]
                if step < 3:
                    for a in range(3):
                        uacc[a, :, lanes] = sums[a]
                else:
                    send_sums(k, half, near, sums, riding)
        return collect(k)

    def collect(k):
        whole(several(rsr, k, 0, GROUP - 1), rs_send.at[k], rs_recv.at[k]).wait_recv()
        parts = [rss[k, p]] + [rsr[k, (p + d) % GROUP] for d in range(1, GROUP)]
        while len(parts) > 1:
            parts = [parts[i] + parts[i + 1] for i in range(0, len(parts), 2)]
        return parts[0]

    def send_packet(k, vector, dots):
        value = jnp.where(body_lanes, vector, 0.0)
        for i, dot in enumerate(dots):
            value = jnp.where(wide == 3 * PAN + i, dot, value)
        pkt[k] = value
        ag[k, q] = value
        for d in FAR_FIRST:
            ag_copy(k, d, q).start()

    def inner(a, b):
        return jnp.sum(jnp.where(body_lanes, a * b, 0.0), axis=1, keepdims=True)

    def pick(total, i):
        return total[:, 3 * PAN + i : 3 * PAN + i + 1]

    def length_of(square, whole):
        return jnp.sqrt(jnp.maximum(square, whole * 1e-7))

    own = jnp.where(body_lanes, pkt[0], 0.0)
    line = jnp.concatenate([self_ref[...], self_ref[...]], axis=1)
    line = jnp.broadcast_to(jnp.concatenate([line, line], axis=1), (8, 2 * TILE))
    self_term = jnp.where(body_lanes, line, 0.0)

    total = apply(0)
    start_norm = jnp.sqrt(pick(total, 0))
    basis0 = own / start_norm
    image0 = (self_term * own + total) / start_norm

    send_packet(1, image0, [inner(basis0, image0), inner(image0, image0)])
    total = apply(1)
    h00 = pick(total, 0)
    square = pick(total, 1)
    h10 = length_of(square - h00 * h00, square)
    basis1 = (image0 - h00 * basis0) / h10
    image1 = (self_term * image0 + total - h00 * image0) / h10

    send_packet(
        2,
        image1,
        [inner(basis1, basis1), inner(basis0, image1), inner(basis1, image1), inner(image1, image1)],
    )
    total = apply(2)
    scale = jnp.sqrt(pick(total, 0))
    second_image = (self_term * image1 + total) / scale
    basis1 = basis1 / scale
    image1 = image1 / scale
    h10 = h10 * scale
    h01 = pick(total, 1) / scale
    h11 = pick(total, 2) / (scale * scale)
    square = pick(total, 3) / (scale * scale)
    h21 = length_of(square - h01 * h01 - h11 * h11, square)
    basis2 = (image1 - h01 * basis0 - h11 * basis1) / h21
    image2 = (second_image - h01 * image0 - h11 * image1) / h21

    send_packet(
        3,
        image2,
        [
            inner(basis2, basis2),
            inner(basis0, image2),
            inner(basis1, image2),
            inner(basis2, image2),
            inner(image2, image2),
        ],
    )
    for shift in range(4):
        wait_shards(3, (own_rows + shift) % 4 if shift else None)
    riding = group_dots(3)
    for d in range(GROUP):
        rss[3, d, :, TILE:] = riding
    for d in FAR_FIRST:
        rs_copy(3, (p + d) % GROUP, p).start()
    total = collect(3)
    scale = jnp.sqrt(pick(total, 0))
    basis2 = basis2 / scale
    h21 = h21 * scale
    h02 = pick(total, 1) / scale
    h12 = pick(total, 2) / scale
    h22 = pick(total, 3) / (scale * scale)
    square = pick(total, 4) / (scale * scale)
    h32 = jnp.sqrt(jnp.maximum(square - h02 * h02 - h12 * h12 - h22 * h22, 0.0))

    columns = [[h00, h10], [h01, h11, h21], [h02, h12, h22, h32]]
    target = [start_norm] + [jnp.zeros_like(start_norm)] * ITERS
    turns = []
    for k in range(ITERS):
        column = columns[k]
        for j in range(k):
            cosine, sine = turns[j]
            column[j], column[j + 1] = (
                cosine * column[j] + sine * column[j + 1],
                cosine * column[j + 1] - sine * column[j],
            )
        radius = jnp.sqrt(column[k] * column[k] + column[k + 1] * column[k + 1])
        cosine, sine = column[k] / radius, column[k + 1] / radius
        turns.append((cosine, sine))
        column[k] = radius
        target[k + 1] = -sine * target[k]
        target[k] = cosine * target[k]
    coeffs = [None] * ITERS
    for k in range(ITERS - 1, -1, -1):
        accum = target[k]
        for i in range(k + 1, ITERS):
            accum = accum - columns[i][k] * coeffs[i]
        coeffs[k] = accum / columns[k][k]
    density = coeffs[0] * basis0 + coeffs[1] * basis1 + coeffs[2] * basis2
    out_ref[:, 0, :] = density[:6, :PAN]
    out_ref[:, 1, :] = density[:6, PAN : 2 * PAN]
    out_ref[:, 2, :] = density[:6, 2 * PAN : 3 * PAN]

    for copy in near_copies():
        copy.wait_send()
    whole(several(rss, 0, 0, GROUP - 1), pts_send.at[0], pts_recv.at[0]).wait_send()
    for k in range(ROUNDS):
        whole(several(rss, k, 0, GROUP - 1), ag_send.at[k], ag_recv.at[k, 0]).wait_send()
        whole(several(rss, k, 0, GROUP - 1), rs_send.at[k], rs_recv.at[k]).wait_send()


def body(velocity, points, panel_area, self_term, near_index, near_weight):
    vmem = pl.BlockSpec(memory_space=pltpu.VMEM)
    rhs = velocity.shape[0]
    return pl.pallas_call(
        kernel,
        out_shape=jax.ShapeDtypeStruct((rhs, 3, PAN), jnp.float32),
        in_specs=[pl.BlockSpec(memory_space=pl.ANY)] * 6,
        out_specs=vmem,
        scratch_shapes=[
            pltpu.VMEM((rhs, 3, PAN), jnp.float32),
            pltpu.VMEM((3, PAN), jnp.float32),
            pltpu.VMEM((1, PAN), jnp.float32),
            pltpu.VMEM((1, PAN), jnp.float32),
            pltpu.VMEM((LISTED, 512), jnp.int32),
            pltpu.VMEM((LISTED, 512), jnp.float32),
            pltpu.VMEM((ROUNDS, 8, 4 * PAN), jnp.float32),
            pltpu.VMEM((ROUNDS, GROUP, 8, 4 * PAN), jnp.float32),
            pltpu.VMEM((GROUP, 8, 4 * PAN), jnp.float32),
            pltpu.VMEM((ROUNDS, GROUP, 8, 4 * PAN), jnp.float32),
            pltpu.VMEM((ROUNDS, GROUP, 8, 4 * PAN), jnp.float32),
            pltpu.VMEM((LISTED, 512), jnp.int32),
            pltpu.VMEM((LISTED, 512), jnp.float32),
            pltpu.VMEM((LISTED, 32, TILE), jnp.float32),
            pltpu.VMEM((LISTED, 32, TILE), jnp.float32),
            pltpu.VMEM((4, LOCAL, TILE), jnp.float32),
            pltpu.VMEM((3, 16, LOCAL), jnp.float32),
            pltpu.VMEM((8, LOCAL, TILE), jnp.float32),
            pltpu.VMEM((BLOCKS, 8, LOCAL + PAD, TILE), jnp.bfloat16),
            pltpu.VMEM((3, 8, LOCAL), jnp.float32),
            pltpu.SemaphoreType.DMA((ROUNDS,)),
            pltpu.SemaphoreType.DMA((ROUNDS, 4)),
            pltpu.SemaphoreType.DMA((1,)),
            pltpu.SemaphoreType.DMA((1,)),
            pltpu.SemaphoreType.DMA((ROUNDS,)),
            pltpu.SemaphoreType.DMA((ROUNDS,)),
            pltpu.SemaphoreType.DMA((2,)),
            pltpu.SemaphoreType.DMA((2,)),
            pltpu.SemaphoreType.DMA((6,)),
        ],
        compiler_params=pltpu.CompilerParams(
            collective_id=0, has_side_effects=True, vmem_limit_bytes=56 * 1024 * 1024
        ),
    )(
        velocity,
        points,
        panel_area.reshape(1, PAN),
        self_term.reshape(1, PAN),
        near_index.T,
        near_weight.T,
    )


def solution(mesh):
    return jax.shard_map(
        body,
        mesh=mesh,
        in_specs=(
            P(None, None, ("row", "col")),
            P(None, ("row", "col")),
            P(("row", "col")),
            P(("row", "col")),
            P("row", "col"),
            P("row", "col"),
        ),
        out_specs=P(None, None, ("row", "col")),
        check_vma=False,
    )
```

```python
import itertools
import math

import jax
import jax.numpy as jnp
from jax import lax
from jax.experimental import pallas as pl
from jax.experimental.pallas import tpu as pltpu
from jax.sharding import PartitionSpec as P

MESH = pl.DeviceIdType.MESH
ITERS = 3
BLOB_SQ = 0.0025
INV_EIGHT_PI = 1.0 / (8.0 * math.pi)
GROUP = 16
PAN = 64
LOCAL = GROUP * PAN
LISTED = 16
MIXED = ((0, 1, 5), (0, 2, 6), (1, 2, 7))
BLOCKS = 8
ORDER = (0, 3, 1, 2)
FAR_FIRST = (8, 9, 7, 6, 10, 5, 11, 4, 12, 3, 13, 2, 14, 1, 15)
CHUNK = 256
HALF = 512
PAD = 16
ROWS = 6
TILE = 128
ROUNDS = ITERS + 1
EARLY = 3


def kernel(
    vel_hbm,
    points_hbm,
    area_hbm,
    self_hbm,
    nidx_hbm,
    nwt_hbm,
    out_ref,
    vel_ref,
    points_ref,
    area_ref,
    self_ref,
    nidx_ref,
    nwt_ref,
    pkt,
    ag,
    pts,
    rss,
    rsr,
    far_idx,
    far_wt,
    digit_a,
    digit_b,
    srcb,
    tgtb,
    nmat,
    wts,
    uacc,
    raw,
    lhs,
    ag_send,
    ag_recv,
    pts_send,
    pts_recv,
    rs_send,
    rs_recv,
    near_send,
    near_recv,
    load_sem,
):
    row = lax.axis_index("row")
    col = lax.axis_index("col")
    y_hi = row // GROUP
    q = row % GROUP
    p = y_hi * 8 + col
    own_rows = q // 4

    def gather_device(other):
        return (y_hi * GROUP + other, col)

    def reduce_device(other):
        return ((other // 8) * GROUP + q, other % 8)

    barrier = pltpu.get_barrier_semaphore()
    for d in range(1, GROUP):
        pl.semaphore_signal(barrier, inc=1, device_id=gather_device((q + d) % GROUP), device_id_type=MESH)
        pl.semaphore_signal(barrier, inc=1, device_id=reduce_device((p + d) % GROUP), device_id_type=MESH)

    loads = [
        pltpu.make_async_copy(outer, inner, load_sem.at[i])
        for i, (outer, inner) in enumerate(
            (
                (nidx_hbm, nidx_ref),
                (nwt_hbm, nwt_ref),
                (vel_hbm, vel_ref),
                (points_hbm, points_ref),
                (area_hbm, area_ref),
                (self_hbm, self_ref),
            )
        )
    ]
    for load in loads:
        load.start()
    for load in loads:
        load.wait()

    spare = [points_ref[0:1], points_ref[1:2], points_ref[2:3], area_ref[...], jnp.zeros((2, PAN), jnp.float32)]
    pkt[0] = jnp.zeros((8, 2 * TILE), jnp.float32)
    pkt[0, :ROWS, :TILE] = jnp.concatenate([vel_ref[:, 0, :], vel_ref[:, 1, :]], axis=1)
    pkt[0, :ROWS, TILE:] = jnp.concatenate([vel_ref[:, 2, :], jnp.concatenate(spare, axis=0)], axis=1)

    partner = ((1 - y_hi) * GROUP + q, col)

    def near_copies():
        return [
            pltpu.make_async_remote_copy(
                src_ref=mine,
                dst_ref=theirs,
                send_sem=near_send.at[i],
                recv_sem=near_recv.at[i],
                device_id=partner,
                device_id_type=MESH,
            )
            for i, (mine, theirs) in enumerate(((nidx_ref, far_idx), (nwt_ref, far_wt)))
        ]

    def window(ref, k):
        return ref.at[pl.ds(0, ROWS)] if k < ITERS else ref.at[pl.ds(0, ROWS), pl.ds(TILE, TILE)]

    def ag_copy(k, other, slot):
        return pltpu.make_async_remote_copy(
            src_ref=window(pkt.at[k], k),
            dst_ref=window(ag.at[k, slot], k),
            send_sem=ag_send.at[k],
            recv_sem=ag_recv.at[k, own_rows],
            device_id=gather_device(other),
            device_id_type=MESH,
        )

    def send_gather(k):
        for d in range(1, 4):
            ag_copy(k, own_rows * 4 + (q + d) % 4, q).start()
        for shift in (2, 1, 3):
            for d in range(4):
                ag_copy(k, (own_rows + shift) % 4 * 4 + d, q).start()

    def pts_copy(d, slot):
        return pltpu.make_async_remote_copy(
            src_ref=window(pkt.at[0], 0),
            dst_ref=window(pts.at[slot], 0),
            send_sem=pts_send.at[0],
            recv_sem=pts_recv.at[0],
            device_id=reduce_device((p + d) % GROUP),
            device_id_type=MESH,
        )

    def rs_copy(k, other, slot):
        return pltpu.make_async_remote_copy(
            src_ref=window(rss.at[k, other], k),
            dst_ref=window(rsr.at[k, slot], k),
            send_sem=rs_send.at[k],
            recv_sem=rs_recv.at[k],
            device_id=reduce_device(other),
            device_id_type=MESH,
        )

    def whole(ref, send, recv):
        return pltpu.make_async_remote_copy(
            src_ref=ref,
            dst_ref=ref,
            send_sem=send,
            recv_sem=recv,
            device_id=partner,
            device_id_type=MESH,
        )

    def several(ref, k, first, count):
        if k < ITERS:
            return ref.at[k, pl.ds(first, count), pl.ds(0, ROWS)]
        return ref.at[k, pl.ds(first, count), pl.ds(0, ROWS), pl.ds(TILE, TILE)]

    digit = lax.broadcasted_iota(jnp.int32, (32, TILE), 0)

    def near_tiles(idx_ref, wt_ref, half, first, count):
        def one(step, carry):
            tile = first + step
            lanes = pl.ds(pl.multiple_of(tile * TILE, TILE), TILE)
            for k in range(LISTED):
                place = idx_ref[k : k + 1, lanes] - y_hi * LOCAL
                weight = wt_ref[k : k + 1, lanes]
                digit_a[k] = jnp.where(digit == lax.shift_right_arithmetic(place, 5), weight, 0.0)
                digit_b[k] = jnp.where(digit == (place & 31), 1.0, 0.0)
            for group in range(4):
                ones = [digit_b[k, group * 8 : group * 8 + 8, :] for k in range(LISTED)]

                def line(step, carry):
                    for u in range(16):
                        top = step * 16 + u
                        parts = [digit_a[k, pl.ds(top, 1), :] * ones[k] for k in range(LISTED)]
                        while len(parts) > 1:
                            parts = [parts[i] + parts[i + 1] for i in range(0, len(parts), 2)]
                        nmat[half * 4 + tile, pl.ds(pl.multiple_of(top * 32 + group * 8, 8), 8), :] = parts[0]
                    return carry

                lax.fori_loop(0, 2, line, 0)
            return carry

        lax.fori_loop(0, count, one, 0)

    near_tiles(nidx_ref, nwt_ref, y_hi, 0, EARLY)
    pl.semaphore_wait(barrier, 2 * (GROUP - 1))

    for copy in near_copies():
        copy.start()
    for d in FAR_FIRST:
        pts_copy(d, p).start()
    send_gather(0)
    ag[0, q] = pkt[0]
    pts[p] = pkt[0]

    near_tiles(nidx_ref, nwt_ref, y_hi, EARLY, 4 - EARLY)
    for copy in near_copies():
        copy.wait_recv()
    near_tiles(far_idx, far_wt, 1 - y_hi, 0, 4)

    lane = lax.broadcasted_iota(jnp.int32, (8, TILE), 1)
    low = lane < PAN
    wide = lax.broadcasted_iota(jnp.int32, (8, 2 * TILE), 1)
    body_lanes = wide < 3 * PAN

    def swap(x):
        return pltpu.roll(x, PAN, 1)

    def join(first, second):
        a, c = first[:, :TILE], first[:, TILE:]
        b, e = second[:, :TILE], second[:, TILE:]
        return (
            jnp.where(low, a, swap(b)),
            jnp.where(low, swap(a), b),
            jnp.where(low, c, swap(e)),
        )

    whole(pts.at[pl.ds(0, GROUP - 1), pl.ds(0, ROWS)], pts_send.at[0], pts_recv.at[0]).wait_recv()
    for m in range(GROUP // 2):
        tile = jnp.where(low, swap(pts[2 * m, :, TILE:]), pts[2 * m + 1, :, TILE:])
        for a in range(3):
            tgtb[a, :, m * TILE : (m + 1) * TILE] = jnp.broadcast_to(tile[a : a + 1], (16, TILE))

    def wait_shards(k, rows):
        count = 3 if rows is None else 4
        rows = own_rows if rows is None else rows
        whole(several(ag, k, rows * 4, count), ag_send.at[k], ag_recv.at[k, rows]).wait_recv()

    def spread_sources(rows):
        for i in range(4):
            s = rows * 4 + i
            place = pl.ds(pl.multiple_of(s * PAN, PAN), PAN)
            tile = ag[0, s, :, TILE:]
            moved = swap(tile)
            for pair in range(2):
                line = jnp.where(low[:1], moved[2 * pair : 2 * pair + 1], tile[2 * pair + 1 : 2 * pair + 2])
                flipped = jnp.transpose(jnp.broadcast_to(line, (TILE, TILE)))
                srcb[2 * pair, place] = flipped[:PAN]
                srcb[2 * pair + 1, place] = flipped[PAN:] if pair == 0 else flipped[PAN:] * INV_EIGHT_PI

    def build(quarter, half, earlier):
        def one(step, carry):
            if earlier is not None:
                old_quarter, old_half, slot = earlier
                old_rows = pl.ds(pl.multiple_of(old_quarter * CHUNK, CHUNK), CHUNK)
                old_lanes = pl.ds(pl.multiple_of(old_half * HALF, HALF), HALF)
                tiles = [wts[step, old_half * (HALF // TILE) + t, old_rows, :] for t in range(HALF // TILE)]
                raw[:, old_lanes] = raw[:, old_lanes] + jnp.dot(
                    lhs[slot, step], jnp.concatenate(tiles, axis=1), preferred_element_type=jnp.float32
                )
            for line, t in itertools.product(range(2), range(HALF // TILE)):
                rows = pl.ds(pl.multiple_of(quarter * CHUNK + step * 32 + line * 16, 16), 16)
                source = [srcb[i, rows, :] for i in range(4)]
                tile = half * (HALF // TILE) + t
                lanes = pl.ds(pl.multiple_of(tile * TILE, TILE), TILE)
                off = [tgtb[a, :, lanes] - source[a] for a in range(3)]
                dist = (off[0] * off[0] + off[1] * off[1]) + (off[2] * off[2] + BLOB_SQ)
                inv = lax.rsqrt(dist)
                two = (source[3] * inv) * (inv * inv)
                near = (dist + BLOB_SQ) * two + nmat[tile, rows, :]
                high = near.astype(jnp.bfloat16)
                wts[0, tile, rows, :] = high
                wts[1, tile, rows, :] = (near - high.astype(jnp.float32)).astype(jnp.bfloat16)
                scaled = [two * v for v in off]
                for a in range(3):
                    wts[2 + a, tile, rows, :] = (scaled[a] * off[a]).astype(jnp.bfloat16)
                for a, b, block in MIXED:
                    wts[block, tile, rows, :] = (scaled[a] * off[b]).astype(jnp.bfloat16)
            return carry

        lax.fori_loop(0, CHUNK // 32, one, 0)

    def fields(k, rows):
        tiles = [join(ag[k, rows * 4 + 2 * m], ag[k, rows * 4 + 2 * m + 1]) for m in range(2)]
        out = []
        for a in range(3):
            value = jnp.concatenate([tiles[0][a], tiles[1][a]], axis=1)
            high = value.astype(jnp.bfloat16).astype(jnp.float32)
            out.append(jnp.concatenate([high, value - high], axis=0).astype(jnp.bfloat16))
        return out

    def products(field, quarter, half):
        rows = pl.ds(pl.multiple_of(quarter * CHUNK, CHUNK), CHUNK)

        def dot(lhs, block):
            tiles = [wts[block, half * (HALF // TILE) + t, rows, :] for t in range(HALF // TILE)]
            return jnp.dot(lhs, jnp.concatenate(tiles, axis=1), preferred_element_type=jnp.float32)

        stacked = jnp.concatenate(field, axis=0)
        both = dot(stacked, 0) + dot(stacked, 1)
        acc = [both[16 * a : 16 * a + 16] + dot(field[a], 2 + a) for a in range(3)]
        for a, b, block in MIXED:
            both = dot(jnp.concatenate([field[a], field[b]], axis=0), block)
            acc[b] = acc[b] + both[:16]
            acc[a] = acc[a] + both[16:]
        return [v[:8] + v[8:] for v in acc]

    def group_dots(k):
        if k == 0:
            total = jnp.zeros((8, 2 * TILE), jnp.float32)
            for s in range(GROUP):
                total = total + ag[0, s] * ag[0, s]
            return jnp.broadcast_to(jnp.sum(jnp.where(body_lanes, total, 0.0), axis=1, keepdims=True), (8, TILE))
        total = ag[k, 0, :, TILE:]
        for s in range(1, GROUP):
            total = total + ag[k, s, :, TILE:]
        return total

    def send_sums(k, half, near, sums, riding):
        for i in range(8):
            t, odd = i // 2, i % 2
            first, second, third = [v[:, t * TILE : (t + 1) * TILE] for v in sums]
            if odd:
                first, third = swap(first), swap(third)
            else:
                second = swap(second)
            other = half * 8 + i
            rss[k, other, :, :TILE] = jnp.where(low, first, second)
            rss[k, other, :, TILE:] = jnp.where(low, third, riding)
        for i in range(8):
            other = half * 8 + i
            if near:

                @pl.when(other != p)
                def _():
                    rs_copy(k, other, p).start()

            else:
                rs_copy(k, other, p).start()

    def fold(half):
        lanes = pl.ds(pl.multiple_of(half * HALF, HALF), HALF)
        return [raw[16 * a : 16 * a + 8, lanes] + raw[16 * a + 8 : 16 * a + 16, lanes] for a in range(3)]

    def fill_lhs(field, slot):
        zero = jnp.zeros((16, CHUNK), jnp.bfloat16)
        lhs[slot, 0] = jnp.concatenate(field, axis=0)
        lhs[slot, 1] = jnp.concatenate(field, axis=0)
        for a in range(3):
            rows = [zero] * 3
            rows[a] = field[a]
            lhs[slot, 2 + a] = jnp.concatenate(rows, axis=0)
        for a, b, block in MIXED:
            rows = [zero] * 3
            rows[a], rows[b] = field[b], field[a]
            lhs[slot, block] = jnp.concatenate(rows, axis=0)

    def first_apply():
        raw[...] = jnp.zeros((48, LOCAL), jnp.float32)
        earlier = None
        for step, shift in enumerate(ORDER):
            quarter = (own_rows + shift) % 4
            wait_shards(0, quarter if shift else None)
            spread_sources(quarter)
            field = fields(0, quarter)
            if step < 3:
                fill_lhs(field, step % 2)
                for near in range(2):
                    half = y_hi if near else 1 - y_hi
                    build(quarter, half, earlier)
                    earlier = (quarter, half, step % 2)
                continue
            riding = group_dots(0)
            for near in range(2):
                half = y_hi if near else 1 - y_hi
                build(quarter, half, earlier)
                earlier = None
                sums = products(field, quarter, half)
                sums = [old + new for old, new in zip(fold(half), sums)]
                send_sums(0, half, near, sums, riding)
        return collect(0)

    def apply(k):
        riding = None
        for step, shift in enumerate(ORDER):
            quarter = (own_rows + shift) % 4
            wait_shards(k, quarter if shift else None)
            field = fields(k, quarter)
            if step == 3:
                riding = group_dots(k)
            for near in range(2):
                half = y_hi if near else 1 - y_hi
                sums = products(field, quarter, half)
                lanes = pl.ds(pl.multiple_of(half * HALF, HALF), HALF)
                if step > 0:
                    sums = [uacc[a, :, lanes] + sums[a] for a in range(3)]
                if step < 3:
                    for a in range(3):
                        uacc[a, :, lanes] = sums[a]
                else:
                    send_sums(k, half, near, sums, riding)
        return collect(k)

    def collect(k):
        whole(several(rsr, k, 0, GROUP - 1), rs_send.at[k], rs_recv.at[k]).wait_recv()
        parts = [rss[k, p]] + [rsr[k, (p + d) % GROUP] for d in range(1, GROUP)]
        while len(parts) > 1:
            parts = [parts[i] + parts[i + 1] for i in range(0, len(parts), 2)]
        return parts[0]

    def send_packet(k, vector, dots):
        value = jnp.where(body_lanes, vector, 0.0)
        for i, dot in enumerate(dots):
            value = jnp.where(wide == 3 * PAN + i, dot, value)
        pkt[k] = value
        ag[k, q] = value
        send_gather(k)

    def inner(a, b):
        return jnp.sum(jnp.where(body_lanes, a * b, 0.0), axis=1, keepdims=True)

    def pick(total, i):
        return total[:, 3 * PAN + i : 3 * PAN + i + 1]

    def length_of(square, whole):
        return jnp.sqrt(jnp.maximum(square, whole * 1e-7))

    own = jnp.where(body_lanes, pkt[0], 0.0)
    line = jnp.concatenate([self_ref[...], self_ref[...]], axis=1)
    line = jnp.broadcast_to(jnp.concatenate([line, line], axis=1), (8, 2 * TILE))
    self_term = jnp.where(body_lanes, line, 0.0)

    total = first_apply()
    start_norm = jnp.sqrt(pick(total, 0))
    basis0 = own / start_norm
    image0 = (self_term * own + total) / start_norm

    send_packet(1, image0, [inner(basis0, image0), inner(image0, image0)])
    total = apply(1)
    h00 = pick(total, 0)
    square = pick(total, 1)
    h10 = length_of(square - h00 * h00, square)
    basis1 = (image0 - h00 * basis0) / h10
    image1 = (self_term * image0 + total - h00 * image0) / h10

    send_packet(
        2,
        image1,
        [inner(basis1, basis1), inner(basis0, image1), inner(basis1, image1), inner(image1, image1)],
    )
    total = apply(2)
    scale = jnp.sqrt(pick(total, 0))
    second_image = (self_term * image1 + total) / scale
    basis1 = basis1 / scale
    image1 = image1 / scale
    h10 = h10 * scale
    h01 = pick(total, 1) / scale
    h11 = pick(total, 2) / (scale * scale)
    square = pick(total, 3) / (scale * scale)
    h21 = length_of(square - h01 * h01 - h11 * h11, square)
    basis2 = (image1 - h01 * basis0 - h11 * basis1) / h21
    image2 = (second_image - h01 * image0 - h11 * image1) / h21

    send_packet(
        3,
        image2,
        [
            inner(basis2, basis2),
            inner(basis0, image2),
            inner(basis1, image2),
            inner(basis2, image2),
            inner(image2, image2),
        ],
    )
    for shift in range(4):
        wait_shards(3, (own_rows + shift) % 4 if shift else None)
    riding = group_dots(3)
    for d in range(GROUP):
        rss[3, d, :, TILE:] = riding
    for d in FAR_FIRST:
        rs_copy(3, (p + d) % GROUP, p).start()
    total = collect(3)
    scale = jnp.sqrt(pick(total, 0))
    basis2 = basis2 / scale
    h21 = h21 * scale
    h02 = pick(total, 1) / scale
    h12 = pick(total, 2) / scale
    h22 = pick(total, 3) / (scale * scale)
    square = pick(total, 4) / (scale * scale)
    h32 = jnp.sqrt(jnp.maximum(square - h02 * h02 - h12 * h12 - h22 * h22, 0.0))

    columns = [[h00, h10], [h01, h11, h21], [h02, h12, h22, h32]]
    target = [start_norm] + [jnp.zeros_like(start_norm)] * ITERS
    turns = []
    for k in range(ITERS):
        column = columns[k]
        for j in range(k):
            cosine, sine = turns[j]
            column[j], column[j + 1] = (
                cosine * column[j] + sine * column[j + 1],
                cosine * column[j + 1] - sine * column[j],
            )
        radius = jnp.sqrt(column[k] * column[k] + column[k + 1] * column[k + 1])
        cosine, sine = column[k] / radius, column[k + 1] / radius
        turns.append((cosine, sine))
        column[k] = radius
        target[k + 1] = -sine * target[k]
        target[k] = cosine * target[k]
    coeffs = [None] * ITERS
    for k in range(ITERS - 1, -1, -1):
        accum = target[k]
        for i in range(k + 1, ITERS):
            accum = accum - columns[i][k] * coeffs[i]
        coeffs[k] = accum / columns[k][k]
    density = coeffs[0] * basis0 + coeffs[1] * basis1 + coeffs[2] * basis2
    out_ref[:, 0, :] = density[:6, :PAN]
    out_ref[:, 1, :] = density[:6, PAN : 2 * PAN]
    out_ref[:, 2, :] = density[:6, 2 * PAN : 3 * PAN]

    for copy in near_copies():
        copy.wait_send()
    whole(several(rss, 0, 0, GROUP - 1), pts_send.at[0], pts_recv.at[0]).wait_send()
    for k in range(ROUNDS):
        whole(several(rss, k, 0, GROUP - 1), ag_send.at[k], ag_recv.at[k, 0]).wait_send()
        whole(several(rss, k, 0, GROUP - 1), rs_send.at[k], rs_recv.at[k]).wait_send()


def body(velocity, points, panel_area, self_term, near_index, near_weight):
    vmem = pl.BlockSpec(memory_space=pltpu.VMEM)
    rhs = velocity.shape[0]
    return pl.pallas_call(
        kernel,
        out_shape=jax.ShapeDtypeStruct((rhs, 3, PAN), jnp.float32),
        in_specs=[pl.BlockSpec(memory_space=pl.ANY)] * 6,
        out_specs=vmem,
        scratch_shapes=[
            pltpu.VMEM((rhs, 3, PAN), jnp.float32),
            pltpu.VMEM((3, PAN), jnp.float32),
            pltpu.VMEM((1, PAN), jnp.float32),
            pltpu.VMEM((1, PAN), jnp.float32),
            pltpu.VMEM((LISTED, 512), jnp.int32),
            pltpu.VMEM((LISTED, 512), jnp.float32),
            pltpu.VMEM((ROUNDS, 8, 4 * PAN), jnp.float32),
            pltpu.VMEM((ROUNDS, GROUP, 8, 4 * PAN), jnp.float32),
            pltpu.VMEM((GROUP, 8, 4 * PAN), jnp.float32),
            pltpu.VMEM((ROUNDS, GROUP, 8, 4 * PAN), jnp.float32),
            pltpu.VMEM((ROUNDS, GROUP, 8, 4 * PAN), jnp.float32),
            pltpu.VMEM((LISTED, 512), jnp.int32),
            pltpu.VMEM((LISTED, 512), jnp.float32),
            pltpu.VMEM((LISTED, 32, TILE), jnp.float32),
            pltpu.VMEM((LISTED, 32, TILE), jnp.float32),
            pltpu.VMEM((4, LOCAL, TILE), jnp.float32),
            pltpu.VMEM((3, 16, LOCAL), jnp.float32),
            pltpu.VMEM((8, LOCAL, TILE), jnp.float32),
            pltpu.VMEM((BLOCKS, 8, LOCAL + PAD, TILE), jnp.bfloat16),
            pltpu.VMEM((3, 8, LOCAL), jnp.float32),
            pltpu.VMEM((48, LOCAL), jnp.float32),
            pltpu.VMEM((2, BLOCKS, 48, CHUNK), jnp.bfloat16),
            pltpu.SemaphoreType.DMA((ROUNDS,)),
            pltpu.SemaphoreType.DMA((ROUNDS, 4)),
            pltpu.SemaphoreType.DMA((1,)),
            pltpu.SemaphoreType.DMA((1,)),
            pltpu.SemaphoreType.DMA((ROUNDS,)),
            pltpu.SemaphoreType.DMA((ROUNDS,)),
            pltpu.SemaphoreType.DMA((2,)),
            pltpu.SemaphoreType.DMA((2,)),
            pltpu.SemaphoreType.DMA((6,)),
        ],
        compiler_params=pltpu.CompilerParams(
            collective_id=0,
            has_side_effects=True,
            vmem_limit_bytes=56 * 1024 * 1024
        ),
    )(
        velocity,
        points,
        panel_area.reshape(1, PAN),
        self_term.reshape(1, PAN),
        near_index.T,
        near_weight.T,
    )


def solution(mesh):
    return jax.shard_map(
        body,
        mesh=mesh,
        in_specs=(
            P(None, None, ("row", "col")),
            P(None, ("row", "col")),
            P(("row", "col")),
            P(("row", "col")),
            P("row", "col"),
            P("row", "col"),
        ),
        out_specs=P(None, None, ("row", "col")),
        check_vma=False,
    )
```

```python
import itertools
import math

import jax
import jax.numpy as jnp
from jax import lax
from jax.experimental import pallas as pl
from jax.experimental.pallas import tpu as pltpu
from jax.sharding import PartitionSpec as P

MESH = pl.DeviceIdType.MESH
ITERS = 3
BLOB_SQ = 0.0025
INV_EIGHT_PI = 1.0 / (8.0 * math.pi)
GROUP = 16
PAN = 64
LOCAL = GROUP * PAN
LISTED = 16
MIXED = ((0, 1, 5), (0, 2, 6), (1, 2, 7))
BLOCKS = 8
FAR_FIRST = (8, 9, 7, 6, 10, 5, 11, 4, 12, 3, 13, 2, 14, 1, 15)
CHUNK = 256
HALF = 512
PAD = 16
ROWS = 6
TILE = 128
ROUNDS = ITERS + 1
EARLY = 3


def kernel(
    vel_hbm,
    points_hbm,
    area_hbm,
    self_hbm,
    nidx_hbm,
    nwt_hbm,
    out_ref,
    vel_ref,
    points_ref,
    area_ref,
    self_ref,
    nidx_ref,
    nwt_ref,
    pkt,
    ag,
    pts,
    rss,
    rsr,
    far_idx,
    far_wt,
    digit_a,
    digit_b,
    srcb,
    tgtb,
    nmat,
    wts,
    uacc,
    ag_send,
    ag_recv,
    pts_send,
    pts_recv,
    rs_send,
    rs_recv,
    near_send,
    near_recv,
    load_sem,
):
    row = lax.axis_index("row")
    col = lax.axis_index("col")
    y_hi = row // GROUP
    q = row % GROUP
    p = y_hi * 8 + col
    own_rows = q // 4

    def gather_device(other):
        return (y_hi * GROUP + other, col)

    def reduce_device(other):
        return ((other // 8) * GROUP + q, other % 8)

    barrier = pltpu.get_barrier_semaphore()
    for d in range(1, GROUP):
        pl.semaphore_signal(barrier, inc=1, device_id=gather_device((q + d) % GROUP), device_id_type=MESH)
        pl.semaphore_signal(barrier, inc=1, device_id=reduce_device((p + d) % GROUP), device_id_type=MESH)

    loads = [
        pltpu.make_async_copy(outer, inner, load_sem.at[i])
        for i, (outer, inner) in enumerate(
            (
                (nidx_hbm, nidx_ref),
                (nwt_hbm, nwt_ref),
                (vel_hbm, vel_ref),
                (points_hbm, points_ref),
                (area_hbm, area_ref),
                (self_hbm, self_ref),
            )
        )
    ]
    for load in loads:
        load.start()
    for load in loads:
        load.wait()

    spare = [points_ref[0:1], points_ref[1:2], points_ref[2:3], area_ref[...], jnp.zeros((2, PAN), jnp.float32)]
    pkt[0] = jnp.zeros((8, 2 * TILE), jnp.float32)
    pkt[0, :ROWS, :TILE] = jnp.concatenate([vel_ref[:, 0, :], vel_ref[:, 1, :]], axis=1)
    pkt[0, :ROWS, TILE:] = jnp.concatenate([vel_ref[:, 2, :], jnp.concatenate(spare, axis=0)], axis=1)

    partner = ((1 - y_hi) * GROUP + q, col)

    def near_copies():
        return [
            pltpu.make_async_remote_copy(
                src_ref=mine,
                dst_ref=theirs,
                send_sem=near_send.at[i],
                recv_sem=near_recv.at[i],
                device_id=partner,
                device_id_type=MESH,
            )
            for i, (mine, theirs) in enumerate(((nidx_ref, far_idx), (nwt_ref, far_wt)))
        ]

    def window(ref, k):
        return ref.at[pl.ds(0, ROWS)] if k < ITERS else ref.at[pl.ds(0, ROWS), pl.ds(TILE, TILE)]

    def ag_copy(k, other, slot):
        return pltpu.make_async_remote_copy(
            src_ref=window(pkt.at[k], k),
            dst_ref=window(ag.at[k, slot], k),
            send_sem=ag_send.at[k],
            recv_sem=ag_recv.at[k, own_rows],
            device_id=gather_device(other),
            device_id_type=MESH,
        )

    def send_gather(k):
        for d in range(1, 4):
            ag_copy(k, own_rows * 4 + (q + d) % 4, q).start()
        for shift in (2, 1, 3):
            for d in range(4):
                ag_copy(k, (own_rows + shift) % 4 * 4 + d, q).start()

    def pts_copy(d, slot):
        return pltpu.make_async_remote_copy(
            src_ref=window(pkt.at[0], ITERS),
            dst_ref=window(pts.at[slot], ITERS),
            send_sem=pts_send.at[0],
            recv_sem=pts_recv.at[0],
            device_id=reduce_device((p + d) % GROUP),
            device_id_type=MESH,
        )

    def rs_copy(k, other, slot):
        return pltpu.make_async_remote_copy(
            src_ref=window(rss.at[k, other], k),
            dst_ref=window(rsr.at[k, slot], k),
            send_sem=rs_send.at[k],
            recv_sem=rs_recv.at[k],
            device_id=reduce_device(other),
            device_id_type=MESH,
        )

    def whole(ref, send, recv):
        return pltpu.make_async_remote_copy(
            src_ref=ref,
            dst_ref=ref,
            send_sem=send,
            recv_sem=recv,
            device_id=partner,
            device_id_type=MESH,
        )

    def several(ref, k, first, count):
        if k < ITERS:
            return ref.at[k, pl.ds(first, count), pl.ds(0, ROWS)]
        return ref.at[k, pl.ds(first, count), pl.ds(0, ROWS), pl.ds(TILE, TILE)]

    digit = lax.broadcasted_iota(jnp.int32, (32, TILE), 0)

    def near_tiles(idx_ref, wt_ref, half, first, count):
        def one(step, carry):
            tile = first + step
            lanes = pl.ds(pl.multiple_of(tile * TILE, TILE), TILE)
            for k in range(LISTED):
                place = idx_ref[k : k + 1, lanes] - y_hi * LOCAL
                weight = wt_ref[k : k + 1, lanes]
                digit_a[k] = jnp.where(digit == lax.shift_right_arithmetic(place, 5), weight, 0.0)
                digit_b[k] = jnp.where(digit == (place & 31), 1.0, 0.0)
            for group in range(4):
                ones = [digit_b[k, group * 8 : group * 8 + 8, :] for k in range(LISTED)]

                def line(step, carry):
                    for u in range(16):
                        top = step * 16 + u
                        parts = [digit_a[k, pl.ds(top, 1), :] * ones[k] for k in range(LISTED)]
                        while len(parts) > 1:
                            parts = [parts[i] + parts[i + 1] for i in range(0, len(parts), 2)]
                        nmat[half * 4 + tile, pl.ds(pl.multiple_of(top * 32 + group * 8, 8), 8), :] = parts[0]
                    return carry

                lax.fori_loop(0, 2, line, 0)
            return carry

        lax.fori_loop(0, count, one, 0)

    near_tiles(nidx_ref, nwt_ref, y_hi, 0, EARLY)
    pl.semaphore_wait(barrier, 2 * (GROUP - 1))

    for copy in near_copies():
        copy.start()
    for d in FAR_FIRST:
        pts_copy(d, p).start()
    send_gather(0)
    ag[0, q] = pkt[0]
    pts[p] = pkt[0]

    near_tiles(nidx_ref, nwt_ref, y_hi, EARLY, 4 - EARLY)
    for copy in near_copies():
        copy.wait_recv()
    near_tiles(far_idx, far_wt, 1 - y_hi, 0, 4)

    lane = lax.broadcasted_iota(jnp.int32, (8, TILE), 1)
    low = lane < PAN
    wide = lax.broadcasted_iota(jnp.int32, (8, 2 * TILE), 1)
    body_lanes = wide < 3 * PAN

    def swap(x):
        return pltpu.roll(x, PAN, 1)

    def join(first, second):
        a, c = first[:, :TILE], first[:, TILE:]
        b, e = second[:, :TILE], second[:, TILE:]
        return (
            jnp.where(low, a, swap(b)),
            jnp.where(low, swap(a), b),
            jnp.where(low, c, swap(e)),
        )

    whole(pts.at[pl.ds(0, GROUP - 1), pl.ds(0, ROWS), pl.ds(TILE, TILE)], pts_send.at[0], pts_recv.at[0]).wait_recv()
    for m in range(GROUP // 2):
        tile = jnp.where(low, swap(pts[2 * m, :, TILE:]), pts[2 * m + 1, :, TILE:])
        for a in range(3):
            tgtb[a, :, m * TILE : (m + 1) * TILE] = jnp.broadcast_to(tile[a : a + 1], (16, TILE))

    def wait_shards(k, rows):
        count = 3 if rows is None else 4
        rows = own_rows if rows is None else rows
        whole(several(ag, k, rows * 4, count), ag_send.at[k], ag_recv.at[k, rows]).wait_recv()

    def spread_sources(rows):
        for i in range(4):
            s = rows * 4 + i
            place = pl.ds(pl.multiple_of(s * PAN, PAN), PAN)
            tile = ag[0, s, :, TILE:]
            moved = swap(tile)
            for pair in range(2):
                line = jnp.where(low[:1], moved[2 * pair : 2 * pair + 1], tile[2 * pair + 1 : 2 * pair + 2])
                flipped = jnp.transpose(jnp.broadcast_to(line, (TILE, TILE)))
                srcb[2 * pair, place] = flipped[:PAN]
                srcb[2 * pair + 1, place] = flipped[PAN:] if pair == 0 else flipped[PAN:] * INV_EIGHT_PI

    def build(quarter, half):
        def one(step, carry):
            for line, t in itertools.product(range(2), range(HALF // TILE)):
                rows = pl.ds(pl.multiple_of(quarter * CHUNK + step * 32 + line * 16, 16), 16)
                source = [srcb[i, rows, :] for i in range(4)]
                tile = half * (HALF // TILE) + t
                lanes = pl.ds(pl.multiple_of(tile * TILE, TILE), TILE)
                off = [tgtb[a, :, lanes] - source[a] for a in range(3)]
                dist = (off[0] * off[0] + off[1] * off[1]) + (off[2] * off[2] + BLOB_SQ)
                inv = lax.rsqrt(dist)
                two = (source[3] * inv) * (inv * inv)
                near = (dist + BLOB_SQ) * two + nmat[tile, rows, :]
                high = near.astype(jnp.bfloat16)
                wts[0, tile, rows, :] = high
                wts[1, tile, rows, :] = (near - high.astype(jnp.float32)).astype(jnp.bfloat16)
                scaled = [two * v for v in off]
                for a in range(3):
                    wts[2 + a, tile, rows, :] = (scaled[a] * off[a]).astype(jnp.bfloat16)
                for a, b, block in MIXED:
                    wts[block, tile, rows, :] = (scaled[a] * off[b]).astype(jnp.bfloat16)
            return carry

        lax.fori_loop(0, CHUNK // 32, one, 0)

    def fields(k, rows):
        tiles = [join(ag[k, rows * 4 + 2 * m], ag[k, rows * 4 + 2 * m + 1]) for m in range(2)]
        out = []
        for a in range(3):
            value = jnp.concatenate([tiles[0][a], tiles[1][a]], axis=1)
            high = value.astype(jnp.bfloat16).astype(jnp.float32)
            out.append(jnp.concatenate([high, value - high], axis=0).astype(jnp.bfloat16))
        return out

    def products(field, quarter, half):
        rows = pl.ds(pl.multiple_of(quarter * CHUNK, CHUNK), CHUNK)

        def dot(lhs, block):
            tiles = [wts[block, half * (HALF // TILE) + t, rows, :] for t in range(HALF // TILE)]
            return jnp.dot(lhs, jnp.concatenate(tiles, axis=1), preferred_element_type=jnp.float32)

        stacked = jnp.concatenate(field, axis=0)
        both = dot(stacked, 0) + dot(stacked, 1)
        acc = [both[16 * a : 16 * a + 16] + dot(field[a], 2 + a) for a in range(3)]
        for a, b, block in MIXED:
            both = dot(jnp.concatenate([field[a], field[b]], axis=0), block)
            acc[b] = acc[b] + both[:16]
            acc[a] = acc[a] + both[16:]
        return [v[:8] + v[8:] for v in acc]

    def group_dots(k):
        if k == 0:
            total = jnp.zeros((8, 2 * TILE), jnp.float32)
            for s in range(GROUP):
                total = total + ag[0, s] * ag[0, s]
            return jnp.broadcast_to(jnp.sum(jnp.where(body_lanes, total, 0.0), axis=1, keepdims=True), (8, TILE))
        total = ag[k, 0, :, TILE:]
        for s in range(1, GROUP):
            total = total + ag[k, s, :, TILE:]
        return total

    def send_sums(k, half, near, sums, riding):
        for i in range(8):
            t, odd = i // 2, i % 2
            first, second, third = [v[:, t * TILE : (t + 1) * TILE] for v in sums]
            if odd:
                first, third = swap(first), swap(third)
            else:
                second = swap(second)
            other = half * 8 + i
            rss[k, other, :, :TILE] = jnp.where(low, first, second)
            rss[k, other, :, TILE:] = jnp.where(low, third, riding)
        for i in range(8):
            other = half * 8 + i
            if near:

                @pl.when(other != p)
                def _():
                    rs_copy(k, other, p).start()

            else:
                rs_copy(k, other, p).start()

    def apply(k):
        riding = None
        for step, shift in enumerate((0, 3, 1, 2)):
            quarter = (own_rows + shift) % 4
            wait_shards(k, quarter if shift else None)
            if k == 0:
                spread_sources(quarter)
            field = fields(k, quarter)
            if step == 3:
                riding = group_dots(k)
            for near in range(2):
                half = y_hi if near else 1 - y_hi
                if k == 0:
                    build(quarter, half)
                sums = products(field, quarter, half)
                lanes = pl.ds(pl.multiple_of(half * HALF, HALF), HALF)
                if step > 0:
                    sums = [uacc[a, :, lanes] + sums[a] for a in range(3)]
                if step < 3:
                    for a in range(3):
                        uacc[a, :, lanes] = sums[a]
                else:
                    send_sums(k, half, near, sums, riding)
        return collect(k)

    def collect(k):
        whole(several(rsr, k, 0, GROUP - 1), rs_send.at[k], rs_recv.at[k]).wait_recv()
        parts = [rss[k, p]] + [rsr[k, (p + d) % GROUP] for d in range(1, GROUP)]
        while len(parts) > 1:
            parts = [parts[i] + parts[i + 1] for i in range(0, len(parts), 2)]
        return parts[0]

    def send_packet(k, vector, dots):
        value = jnp.where(body_lanes, vector, 0.0)
        for i, dot in enumerate(dots):
            value = jnp.where(wide == 3 * PAN + i, dot, value)
        pkt[k] = value
        ag[k, q] = value
        send_gather(k)

    def inner(a, b):
        return jnp.sum(jnp.where(body_lanes, a * b, 0.0), axis=1, keepdims=True)

    def pick(total, i):
        return total[:, 3 * PAN + i : 3 * PAN + i + 1]

    def length_of(square, whole):
        return jnp.sqrt(jnp.maximum(square, whole * 1e-7))

    own = jnp.where(body_lanes, pkt[0], 0.0)
    line = jnp.concatenate([self_ref[...], self_ref[...]], axis=1)
    line = jnp.broadcast_to(jnp.concatenate([line, line], axis=1), (8, 2 * TILE))
    self_term = jnp.where(body_lanes, line, 0.0)

    total = apply(0)
    start_norm = jnp.sqrt(pick(total, 0))
    basis0 = own / start_norm
    image0 = (self_term * own + total) / start_norm

    send_packet(1, image0, [inner(basis0, image0), inner(image0, image0)])
    total = apply(1)
    h00 = pick(total, 0)
    square = pick(total, 1)
    h10 = length_of(square - h00 * h00, square)
    basis1 = (image0 - h00 * basis0) / h10
    image1 = (self_term * image0 + total - h00 * image0) / h10

    send_packet(
        2,
        image1,
        [inner(basis1, basis1), inner(basis0, image1), inner(basis1, image1), inner(image1, image1)],
    )
    total = apply(2)
    scale = jnp.sqrt(pick(total, 0))
    second_image = (self_term * image1 + total) / scale
    basis1 = basis1 / scale
    image1 = image1 / scale
    h10 = h10 * scale
    h01 = pick(total, 1) / scale
    h11 = pick(total, 2) / (scale * scale)
    square = pick(total, 3) / (scale * scale)
    h21 = length_of(square - h01 * h01 - h11 * h11, square)
    basis2 = (image1 - h01 * basis0 - h11 * basis1) / h21
    image2 = (second_image - h01 * image0 - h11 * image1) / h21

    send_packet(
        3,
        image2,
        [
            inner(basis2, basis2),
            inner(basis0, image2),
            inner(basis1, image2),
            inner(basis2, image2),
            inner(image2, image2),
        ],
    )
    for shift in range(4):
        wait_shards(3, (own_rows + shift) % 4 if shift else None)
    riding = group_dots(3)
    for d in range(GROUP):
        rss[3, d, :, TILE:] = riding
    for d in FAR_FIRST:
        rs_copy(3, (p + d) % GROUP, p).start()
    total = collect(3)
    scale = jnp.sqrt(pick(total, 0))
    basis2 = basis2 / scale
    h21 = h21 * scale
    h02 = pick(total, 1) / scale
    h12 = pick(total, 2) / scale
    h22 = pick(total, 3) / (scale * scale)
    square = pick(total, 4) / (scale * scale)
    h32 = jnp.sqrt(jnp.maximum(square - h02 * h02 - h12 * h12 - h22 * h22, 0.0))

    columns = [[h00, h10], [h01, h11, h21], [h02, h12, h22, h32]]
    target = [start_norm] + [jnp.zeros_like(start_norm)] * ITERS
    turns = []
    for k in range(ITERS):
        column = columns[k]
        for j in range(k):
            cosine, sine = turns[j]
            column[j], column[j + 1] = (
                cosine * column[j] + sine * column[j + 1],
                cosine * column[j + 1] - sine * column[j],
            )
        radius = jnp.sqrt(column[k] * column[k] + column[k + 1] * column[k + 1])
        cosine, sine = column[k] / radius, column[k + 1] / radius
        turns.append((cosine, sine))
        column[k] = radius
        target[k + 1] = -sine * target[k]
        target[k] = cosine * target[k]
    coeffs = [None] * ITERS
    for k in range(ITERS - 1, -1, -1):
        accum = target[k]
        for i in range(k + 1, ITERS):
            accum = accum - columns[i][k] * coeffs[i]
        coeffs[k] = accum / columns[k][k]
    density = coeffs[0] * basis0 + coeffs[1] * basis1 + coeffs[2] * basis2
    out_ref[:, 0, :] = density[:6, :PAN]
    out_ref[:, 1, :] = density[:6, PAN : 2 * PAN]
    out_ref[:, 2, :] = density[:6, 2 * PAN : 3 * PAN]

    for copy in near_copies():
        copy.wait_send()
    whole(several(rss, ITERS, 0, GROUP - 1), pts_send.at[0], pts_recv.at[0]).wait_send()
    for k in range(ROUNDS):
        whole(several(rss, k, 0, GROUP - 1), ag_send.at[k], ag_recv.at[k, 0]).wait_send()
        whole(several(rss, k, 0, GROUP - 1), rs_send.at[k], rs_recv.at[k]).wait_send()


def body(velocity, points, panel_area, self_term, near_index, near_weight):
    vmem = pl.BlockSpec(memory_space=pltpu.VMEM)
    rhs = velocity.shape[0]
    return pl.pallas_call(
        kernel,
        out_shape=jax.ShapeDtypeStruct((rhs, 3, PAN), jnp.float32),
        in_specs=[pl.BlockSpec(memory_space=pl.ANY)] * 6,
        out_specs=vmem,
        scratch_shapes=[
            pltpu.VMEM((rhs, 3, PAN), jnp.float32),
            pltpu.VMEM((3, PAN), jnp.float32),
            pltpu.VMEM((1, PAN), jnp.float32),
            pltpu.VMEM((1, PAN), jnp.float32),
            pltpu.VMEM((LISTED, 512), jnp.int32),
            pltpu.VMEM((LISTED, 512), jnp.float32),
            pltpu.VMEM((ROUNDS, 8, 4 * PAN), jnp.float32),
            pltpu.VMEM((ROUNDS, GROUP, 8, 4 * PAN), jnp.float32),
            pltpu.VMEM((GROUP, 8, 4 * PAN), jnp.float32),
            pltpu.VMEM((ROUNDS, GROUP, 8, 4 * PAN), jnp.float32),
            pltpu.VMEM((ROUNDS, GROUP, 8, 4 * PAN), jnp.float32),
            pltpu.VMEM((LISTED, 512), jnp.int32),
            pltpu.VMEM((LISTED, 512), jnp.float32),
            pltpu.VMEM((LISTED, 32, TILE), jnp.float32),
            pltpu.VMEM((LISTED, 32, TILE), jnp.float32),
            pltpu.VMEM((4, LOCAL, TILE), jnp.float32),
            pltpu.VMEM((3, 16, LOCAL), jnp.float32),
            pltpu.VMEM((8, LOCAL, TILE), jnp.float32),
            pltpu.VMEM((BLOCKS, 8, LOCAL + PAD, TILE), jnp.bfloat16),
            pltpu.VMEM((3, 8, LOCAL), jnp.float32),
            pltpu.SemaphoreType.DMA((ROUNDS,)),
            pltpu.SemaphoreType.DMA((ROUNDS, 4)),
            pltpu.SemaphoreType.DMA((1,)),
            pltpu.SemaphoreType.DMA((1,)),
            pltpu.SemaphoreType.DMA((ROUNDS,)),
            pltpu.SemaphoreType.DMA((ROUNDS,)),
            pltpu.SemaphoreType.DMA((2,)),
            pltpu.SemaphoreType.DMA((2,)),
            pltpu.SemaphoreType.DMA((6,)),
        ],
        compiler_params=pltpu.CompilerParams(
            collective_id=0,
            has_side_effects=True,
            vmem_limit_bytes=56 * 1024 * 1024
        ),
    )(
        velocity,
        points,
        panel_area.reshape(1, PAN),
        self_term.reshape(1, PAN),
        near_index.T,
        near_weight.T,
    )


def solution(mesh):
    return jax.shard_map(
        body,
        mesh=mesh,
        in_specs=(
            P(None, None, ("row", "col")),
            P(None, ("row", "col")),
            P(("row", "col")),
            P(("row", "col")),
            P("row", "col"),
            P("row", "col"),
        ),
        out_specs=P(None, None, ("row", "col")),
        check_vma=False,
    )
```

```python
import itertools
import math

import jax
import jax.numpy as jnp
from jax import lax
from jax.experimental import pallas as pl
from jax.experimental.pallas import tpu as pltpu
from jax.sharding import PartitionSpec as P

MESH = pl.DeviceIdType.MESH
ITERS = 3
BLOB_SQ = 0.0025
INV_EIGHT_PI = 1.0 / (8.0 * math.pi)
GROUP = 16
PAN = 64
LOCAL = GROUP * PAN
LISTED = 16
MIXED = ((0, 1, 5), (0, 2, 6), (1, 2, 7))
BLOCKS = 8
FAR_FIRST = (8, 9, 7, 6, 10, 5, 11, 4, 12, 3, 13, 2, 14, 1, 15)
CHUNK = 256
HALF = 512
PAD = 16
ROWS = 6
TILE = 128
ROUNDS = ITERS + 1
EARLY = 2


def kernel(
    vel_hbm,
    points_hbm,
    area_hbm,
    self_hbm,
    nidx_hbm,
    nwt_hbm,
    out_ref,
    vel_ref,
    points_ref,
    area_ref,
    self_ref,
    nidx_ref,
    nwt_ref,
    pkt,
    ag,
    pts,
    rss,
    rsr,
    far_idx,
    far_wt,
    digit_a,
    digit_b,
    srcb,
    tgtb,
    nmat,
    wts,
    uacc,
    ag_send,
    ag_recv,
    pts_send,
    pts_recv,
    rs_send,
    rs_recv,
    near_send,
    near_recv,
    load_sem,
):
    row = lax.axis_index("row")
    col = lax.axis_index("col")
    y_hi = row // GROUP
    q = row % GROUP
    p = y_hi * 8 + col
    own_rows = q // 4

    def gather_device(other):
        return (y_hi * GROUP + other, col)

    def reduce_device(other):
        return ((other // 8) * GROUP + q, other % 8)

    barrier = pltpu.get_barrier_semaphore()
    for d in range(1, GROUP):
        pl.semaphore_signal(barrier, inc=1, device_id=gather_device((q + d) % GROUP), device_id_type=MESH)
        pl.semaphore_signal(barrier, inc=1, device_id=reduce_device((p + d) % GROUP), device_id_type=MESH)

    loads = [
        pltpu.make_async_copy(outer, inner, load_sem.at[i])
        for i, (outer, inner) in enumerate(
            (
                (nidx_hbm, nidx_ref),
                (nwt_hbm, nwt_ref),
                (vel_hbm, vel_ref),
                (points_hbm, points_ref),
                (area_hbm, area_ref),
                (self_hbm, self_ref),
            )
        )
    ]
    for load in loads:
        load.start()
    for load in loads:
        load.wait()

    spare = [points_ref[0:1], points_ref[1:2], points_ref[2:3], area_ref[...], jnp.zeros((2, PAN), jnp.float32)]
    pkt[0] = jnp.zeros((8, 2 * TILE), jnp.float32)
    pkt[0, :ROWS, :TILE] = jnp.concatenate([vel_ref[:, 0, :], vel_ref[:, 1, :]], axis=1)
    pkt[0, :ROWS, TILE:] = jnp.concatenate([vel_ref[:, 2, :], jnp.concatenate(spare, axis=0)], axis=1)

    partner = ((1 - y_hi) * GROUP + q, col)

    def near_copies(tile):
        lanes = pl.ds(tile * TILE, TILE)
        return [
            pltpu.make_async_remote_copy(
                src_ref=mine.at[:, lanes],
                dst_ref=theirs.at[:, lanes],
                send_sem=near_send.at[i, tile],
                recv_sem=near_recv.at[i, tile],
                device_id=partner,
                device_id_type=MESH,
            )
            for i, (mine, theirs) in enumerate(((nidx_ref, far_idx), (nwt_ref, far_wt)))
        ]

    def window(ref, k):
        return ref.at[pl.ds(0, ROWS)] if k < ITERS else ref.at[pl.ds(0, ROWS), pl.ds(TILE, TILE)]

    def ag_copy(k, other, slot):
        return pltpu.make_async_remote_copy(
            src_ref=window(pkt.at[k], k),
            dst_ref=window(ag.at[k, slot], k),
            send_sem=ag_send.at[k],
            recv_sem=ag_recv.at[k, own_rows],
            device_id=gather_device(other),
            device_id_type=MESH,
        )

    def send_gather(k):
        for d in range(1, 4):
            ag_copy(k, own_rows * 4 + (q + d) % 4, q).start()
        for shift in (2, 1, 3):
            for d in range(4):
                ag_copy(k, (own_rows + shift) % 4 * 4 + d, q).start()

    def pts_copy(d, slot):
        return pltpu.make_async_remote_copy(
            src_ref=window(pkt.at[0], ITERS),
            dst_ref=window(pts.at[slot], ITERS),
            send_sem=pts_send.at[0],
            recv_sem=pts_recv.at[0],
            device_id=reduce_device((p + d) % GROUP),
            device_id_type=MESH,
        )

    def rs_copy(k, other, slot):
        return pltpu.make_async_remote_copy(
            src_ref=window(rss.at[k, other], k),
            dst_ref=window(rsr.at[k, slot], k),
            send_sem=rs_send.at[k],
            recv_sem=rs_recv.at[k],
            device_id=reduce_device(other),
            device_id_type=MESH,
        )

    def whole(ref, send, recv):
        return pltpu.make_async_remote_copy(
            src_ref=ref,
            dst_ref=ref,
            send_sem=send,
            recv_sem=recv,
            device_id=partner,
            device_id_type=MESH,
        )

    def several(ref, k, first, count):
        if k < ITERS:
            return ref.at[k, pl.ds(first, count), pl.ds(0, ROWS)]
        return ref.at[k, pl.ds(first, count), pl.ds(0, ROWS), pl.ds(TILE, TILE)]

    digit = lax.broadcasted_iota(jnp.int32, (32, TILE), 0)

    def near_tiles(idx_ref, wt_ref, half, first, count):
        def one(step, carry):
            tile = first + step
            lanes = pl.ds(pl.multiple_of(tile * TILE, TILE), TILE)
            for k in range(LISTED):
                place = idx_ref[k : k + 1, lanes] - y_hi * LOCAL
                weight = wt_ref[k : k + 1, lanes]
                digit_a[k] = jnp.where(digit == lax.shift_right_arithmetic(place, 5), weight, 0.0)
                digit_b[k] = jnp.where(digit == (place & 31), 1.0, 0.0)
            for group in range(4):
                ones = [digit_b[k, group * 8 : group * 8 + 8, :] for k in range(LISTED)]

                def line(step, carry):
                    for u in range(16):
                        top = step * 16 + u
                        parts = [digit_a[k, pl.ds(top, 1), :] * ones[k] for k in range(LISTED)]
                        while len(parts) > 1:
                            parts = [parts[i] + parts[i + 1] for i in range(0, len(parts), 2)]
                        nmat[half * 4 + tile, pl.ds(pl.multiple_of(top * 32 + group * 8, 8), 8), :] = parts[0]
                    return carry

                lax.fori_loop(0, 2, line, 0)
            return carry

        lax.fori_loop(0, count, one, 0)

    near_tiles(nidx_ref, nwt_ref, y_hi, 0, EARLY)
    pl.semaphore_wait(barrier, 2 * (GROUP - 1))

    for tile in range(4):
        for copy in near_copies(tile):
            copy.start()
    for d in FAR_FIRST:
        pts_copy(d, p).start()
    send_gather(0)
    ag[0, q] = pkt[0]
    pts[p] = pkt[0]

    near_tiles(nidx_ref, nwt_ref, y_hi, EARLY, 4 - EARLY)
    for tile in range(4):
        for copy in near_copies(tile):
            copy.wait_recv()
        near_tiles(far_idx, far_wt, 1 - y_hi, tile, 1)

    lane = lax.broadcasted_iota(jnp.int32, (8, TILE), 1)
    low = lane < PAN
    wide = lax.broadcasted_iota(jnp.int32, (8, 2 * TILE), 1)
    body_lanes = wide < 3 * PAN

    def swap(x):
        return pltpu.roll(x, PAN, 1)

    def join(first, second):
        a, c = first[:, :TILE], first[:, TILE:]
        b, e = second[:, :TILE], second[:, TILE:]
        return (
            jnp.where(low, a, swap(b)),
            jnp.where(low, swap(a), b),
            jnp.where(low, c, swap(e)),
        )

    whole(pts.at[pl.ds(0, GROUP - 1), pl.ds(0, ROWS), pl.ds(TILE, TILE)], pts_send.at[0], pts_recv.at[0]).wait_recv()
    for m in range(GROUP // 2):
        tile = jnp.where(low, swap(pts[2 * m, :, TILE:]), pts[2 * m + 1, :, TILE:])
        for a in range(3):
            tgtb[a, :, m * TILE : (m + 1) * TILE] = jnp.broadcast_to(tile[a : a + 1], (16, TILE))

    def wait_shards(k, rows):
        count = 3 if rows is None else 4
        rows = own_rows if rows is None else rows
        whole(several(ag, k, rows * 4, count), ag_send.at[k], ag_recv.at[k, rows]).wait_recv()

    def spread_sources(rows):
        for i in range(4):
            s = rows * 4 + i
            place = pl.ds(pl.multiple_of(s * PAN, PAN), PAN)
            tile = ag[0, s, :, TILE:]
            moved = swap(tile)
            for pair in range(2):
                line = jnp.where(low[:1], moved[2 * pair : 2 * pair + 1], tile[2 * pair + 1 : 2 * pair + 2])
                flipped = jnp.transpose(jnp.broadcast_to(line, (TILE, TILE)))
                srcb[2 * pair, place] = flipped[:PAN]
                srcb[2 * pair + 1, place] = flipped[PAN:] if pair == 0 else flipped[PAN:] * INV_EIGHT_PI

    def build(quarter, half):
        def one(step, carry):
            for line, t in itertools.product(range(2), range(HALF // TILE)):
                rows = pl.ds(pl.multiple_of(quarter * CHUNK + step * 32 + line * 16, 16), 16)
                source = [srcb[i, rows, :] for i in range(4)]
                tile = half * (HALF // TILE) + t
                lanes = pl.ds(pl.multiple_of(tile * TILE, TILE), TILE)
                off = [tgtb[a, :, lanes] - source[a] for a in range(3)]
                dist = (off[0] * off[0] + off[1] * off[1]) + (off[2] * off[2] + BLOB_SQ)
                inv = lax.rsqrt(dist)
                two = (source[3] * inv) * (inv * inv)
                near = (dist + BLOB_SQ) * two + nmat[tile, rows, :]
                high = near.astype(jnp.bfloat16)
                wts[0, tile, rows, :] = high
                wts[1, tile, rows, :] = (near - high.astype(jnp.float32)).astype(jnp.bfloat16)
                scaled = [two * v for v in off]
                for a in range(3):
                    wts[2 + a, tile, rows, :] = (scaled[a] * off[a]).astype(jnp.bfloat16)
                for a, b, block in MIXED:
                    wts[block, tile, rows, :] = (scaled[a] * off[b]).astype(jnp.bfloat16)
            return carry

        lax.fori_loop(0, CHUNK // 32, one, 0)

    def fields(k, rows):
        tiles = [join(ag[k, rows * 4 + 2 * m], ag[k, rows * 4 + 2 * m + 1]) for m in range(2)]
        out = []
        for a in range(3):
            value = jnp.concatenate([tiles[0][a], tiles[1][a]], axis=1)
            high = value.astype(jnp.bfloat16).astype(jnp.float32)
            out.append(jnp.concatenate([high, value - high], axis=0).astype(jnp.bfloat16))
        return out

    def products(field, quarter, half):
        rows = pl.ds(pl.multiple_of(quarter * CHUNK, CHUNK), CHUNK)

        def dot(lhs, block):
            tiles = [wts[block, half * (HALF // TILE) + t, rows, :] for t in range(HALF // TILE)]
            return jnp.dot(lhs, jnp.concatenate(tiles, axis=1), preferred_element_type=jnp.float32)

        stacked = jnp.concatenate(field, axis=0)
        both = dot(stacked, 0) + dot(stacked, 1)
        acc = [both[16 * a : 16 * a + 16] + dot(field[a], 2 + a) for a in range(3)]
        for a, b, block in MIXED:
            both = dot(jnp.concatenate([field[a], field[b]], axis=0), block)
            acc[b] = acc[b] + both[:16]
            acc[a] = acc[a] + both[16:]
        return [v[:8] + v[8:] for v in acc]

    def group_dots(k):
        if k == 0:
            total = jnp.zeros((8, 2 * TILE), jnp.float32)
            for s in range(GROUP):
                total = total + ag[0, s] * ag[0, s]
            return jnp.broadcast_to(jnp.sum(jnp.where(body_lanes, total, 0.0), axis=1, keepdims=True), (8, TILE))
        total = ag[k, 0, :, TILE:]
        for s in range(1, GROUP):
            total = total + ag[k, s, :, TILE:]
        return total

    def send_sums(k, half, near, sums, riding):
        for i in range(8):
            t, odd = i // 2, i % 2
            first, second, third = [v[:, t * TILE : (t + 1) * TILE] for v in sums]
            if odd:
                first, third = swap(first), swap(third)
            else:
                second = swap(second)
            other = half * 8 + i
            rss[k, other, :, :TILE] = jnp.where(low, first, second)
            rss[k, other, :, TILE:] = jnp.where(low, third, riding)
        for i in range(8):
            other = half * 8 + i
            if near:

                @pl.when(other != p)
                def _():
                    rs_copy(k, other, p).start()

            else:
                rs_copy(k, other, p).start()

    def apply(k):
        riding = None
        for step, shift in enumerate((0, 3, 1, 2)):
            quarter = (own_rows + shift) % 4
            wait_shards(k, quarter if shift else None)
            if k == 0:
                spread_sources(quarter)
            field = fields(k, quarter)
            if step == 3:
                riding = group_dots(k)
            for near in range(2):
                half = y_hi if near else 1 - y_hi
                if k == 0:
                    build(quarter, half)
                sums = products(field, quarter, half)
                lanes = pl.ds(pl.multiple_of(half * HALF, HALF), HALF)
                if step > 0:
                    sums = [uacc[a, :, lanes] + sums[a] for a in range(3)]
                if step < 3:
                    for a in range(3):
                        uacc[a, :, lanes] = sums[a]
                else:
                    send_sums(k, half, near, sums, riding)
        return collect(k)

    def collect(k):
        whole(several(rsr, k, 0, GROUP - 1), rs_send.at[k], rs_recv.at[k]).wait_recv()
        parts = [rss[k, p]] + [rsr[k, (p + d) % GROUP] for d in range(1, GROUP)]
        while len(parts) > 1:
            parts = [parts[i] + parts[i + 1] for i in range(0, len(parts), 2)]
        return parts[0]

    def send_packet(k, vector, dots):
        value = jnp.where(body_lanes, vector, 0.0)
        for i, dot in enumerate(dots):
            value = jnp.where(wide == 3 * PAN + i, dot, value)
        pkt[k] = value
        ag[k, q] = value
        send_gather(k)

    def inner(a, b):
        return jnp.sum(jnp.where(body_lanes, a * b, 0.0), axis=1, keepdims=True)

    def pick(total, i):
        return total[:, 3 * PAN + i : 3 * PAN + i + 1]

    def length_of(square, whole):
        return jnp.sqrt(jnp.maximum(square, whole * 1e-7))

    own = jnp.where(body_lanes, pkt[0], 0.0)
    line = jnp.concatenate([self_ref[...], self_ref[...]], axis=1)
    line = jnp.broadcast_to(jnp.concatenate([line, line], axis=1), (8, 2 * TILE))
    self_term = jnp.where(body_lanes, line, 0.0)

    total = apply(0)
    start_norm = jnp.sqrt(pick(total, 0))
    basis0 = own / start_norm
    image0 = (self_term * own + total) / start_norm

    send_packet(1, image0, [inner(basis0, image0), inner(image0, image0)])
    total = apply(1)
    h00 = pick(total, 0)
    square = pick(total, 1)
    h10 = length_of(square - h00 * h00, square)
    basis1 = (image0 - h00 * basis0) / h10
    image1 = (self_term * image0 + total - h00 * image0) / h10

    send_packet(
        2,
        image1,
        [inner(basis1, basis1), inner(basis0, image1), inner(basis1, image1), inner(image1, image1)],
    )
    total = apply(2)
    scale = jnp.sqrt(pick(total, 0))
    second_image = (self_term * image1 + total) / scale
    basis1 = basis1 / scale
    image1 = image1 / scale
    h10 = h10 * scale
    h01 = pick(total, 1) / scale
    h11 = pick(total, 2) / (scale * scale)
    square = pick(total, 3) / (scale * scale)
    h21 = length_of(square - h01 * h01 - h11 * h11, square)
    basis2 = (image1 - h01 * basis0 - h11 * basis1) / h21
    image2 = (second_image - h01 * image0 - h11 * image1) / h21

    send_packet(
        3,
        image2,
        [
            inner(basis2, basis2),
            inner(basis0, image2),
            inner(basis1, image2),
            inner(basis2, image2),
            inner(image2, image2),
        ],
    )
    for shift in range(4):
        wait_shards(3, (own_rows + shift) % 4 if shift else None)
    riding = group_dots(3)
    for d in range(GROUP):
        rss[3, d, :, TILE:] = riding
    for d in FAR_FIRST:
        rs_copy(3, (p + d) % GROUP, p).start()
    total = collect(3)
    scale = jnp.sqrt(pick(total, 0))
    basis2 = basis2 / scale
    h21 = h21 * scale
    h02 = pick(total, 1) / scale
    h12 = pick(total, 2) / scale
    h22 = pick(total, 3) / (scale * scale)
    square = pick(total, 4) / (scale * scale)
    h32 = jnp.sqrt(jnp.maximum(square - h02 * h02 - h12 * h12 - h22 * h22, 0.0))

    columns = [[h00, h10], [h01, h11, h21], [h02, h12, h22, h32]]
    target = [start_norm] + [jnp.zeros_like(start_norm)] * ITERS
    turns = []
    for k in range(ITERS):
        column = columns[k]
        for j in range(k):
            cosine, sine = turns[j]
            column[j], column[j + 1] = (
                cosine * column[j] + sine * column[j + 1],
                cosine * column[j + 1] - sine * column[j],
            )
        radius = jnp.sqrt(column[k] * column[k] + column[k + 1] * column[k + 1])
        cosine, sine = column[k] / radius, column[k + 1] / radius
        turns.append((cosine, sine))
        column[k] = radius
        target[k + 1] = -sine * target[k]
        target[k] = cosine * target[k]
    coeffs = [None] * ITERS
    for k in range(ITERS - 1, -1, -1):
        accum = target[k]
        for i in range(k + 1, ITERS):
            accum = accum - columns[i][k] * coeffs[i]
        coeffs[k] = accum / columns[k][k]
    density = coeffs[0] * basis0 + coeffs[1] * basis1 + coeffs[2] * basis2
    out_ref[:, 0, :] = density[:6, :PAN]
    out_ref[:, 1, :] = density[:6, PAN : 2 * PAN]
    out_ref[:, 2, :] = density[:6, 2 * PAN : 3 * PAN]

    for tile in range(4):
        for copy in near_copies(tile):
            copy.wait_send()
    whole(several(rss, ITERS, 0, GROUP - 1), pts_send.at[0], pts_recv.at[0]).wait_send()
    for k in range(ROUNDS):
        whole(several(rss, k, 0, GROUP - 1), ag_send.at[k], ag_recv.at[k, 0]).wait_send()
        whole(several(rss, k, 0, GROUP - 1), rs_send.at[k], rs_recv.at[k]).wait_send()


def body(velocity, points, panel_area, self_term, near_index, near_weight):
    vmem = pl.BlockSpec(memory_space=pltpu.VMEM)
    rhs = velocity.shape[0]
    return pl.pallas_call(
        kernel,
        out_shape=jax.ShapeDtypeStruct((rhs, 3, PAN), jnp.float32),
        in_specs=[pl.BlockSpec(memory_space=pl.ANY)] * 6,
        out_specs=vmem,
        scratch_shapes=[
            pltpu.VMEM((rhs, 3, PAN), jnp.float32),
            pltpu.VMEM((3, PAN), jnp.float32),
            pltpu.VMEM((1, PAN), jnp.float32),
            pltpu.VMEM((1, PAN), jnp.float32),
            pltpu.VMEM((LISTED, 512), jnp.int32),
            pltpu.VMEM((LISTED, 512), jnp.float32),
            pltpu.VMEM((ROUNDS, 8, 4 * PAN), jnp.float32),
            pltpu.VMEM((ROUNDS, GROUP, 8, 4 * PAN), jnp.float32),
            pltpu.VMEM((GROUP, 8, 4 * PAN), jnp.float32),
            pltpu.VMEM((ROUNDS, GROUP, 8, 4 * PAN), jnp.float32),
            pltpu.VMEM((ROUNDS, GROUP, 8, 4 * PAN), jnp.float32),
            pltpu.VMEM((LISTED, 512), jnp.int32),
            pltpu.VMEM((LISTED, 512), jnp.float32),
            pltpu.VMEM((LISTED, 32, TILE), jnp.float32),
            pltpu.VMEM((LISTED, 32, TILE), jnp.float32),
            pltpu.VMEM((4, LOCAL, TILE), jnp.float32),
            pltpu.VMEM((3, 16, LOCAL), jnp.float32),
            pltpu.VMEM((8, LOCAL, TILE), jnp.float32),
            pltpu.VMEM((BLOCKS, 8, LOCAL + PAD, TILE), jnp.bfloat16),
            pltpu.VMEM((3, 8, LOCAL), jnp.float32),
            pltpu.SemaphoreType.DMA((ROUNDS,)),
            pltpu.SemaphoreType.DMA((ROUNDS, 4)),
            pltpu.SemaphoreType.DMA((1,)),
            pltpu.SemaphoreType.DMA((1,)),
            pltpu.SemaphoreType.DMA((ROUNDS,)),
            pltpu.SemaphoreType.DMA((ROUNDS,)),
            pltpu.SemaphoreType.DMA((2, 4)),
            pltpu.SemaphoreType.DMA((2, 4)),
            pltpu.SemaphoreType.DMA((6,)),
        ],
        compiler_params=pltpu.CompilerParams(
            collective_id=0,
            has_side_effects=True,
            vmem_limit_bytes=56 * 1024 * 1024
        ),
    )(
        velocity,
        points,
        panel_area.reshape(1, PAN),
        self_term.reshape(1, PAN),
        near_index.T,
        near_weight.T,
    )


def solution(mesh):
    return jax.shard_map(
        body,
        mesh=mesh,
        in_specs=(
            P(None, None, ("row", "col")),
            P(None, ("row", "col")),
            P(("row", "col")),
            P(("row", "col")),
            P("row", "col"),
            P("row", "col"),
        ),
        out_specs=P(None, None, ("row", "col")),
        check_vma=False,
    )
```
